32 devices in a mesh: orient: 16 (over z, y, core), frame: 2 (over x).
Axes of the slice: x: 2, y: 2, z: 4, core: 2. Of those that a mesh axis runs over, the one named last changes fastest.
Arguments:
- log_tomograms: bfloat16 [2048, 4096], P('orient'), may hold values from -3 to 3
- frames: int32 [512, 4096], P('frame'), may hold values from 0 to 15, as said below
- tile_index: int32 [2, 32, 2048], P(None, 'frame', 'orient'), may hold values from 0 to 383
- tile_weight: float32 [2, 32, 2048], P(None, 'frame', 'orient'), may hold values from 0.1 to 1
- prior_volume: float32 [2, 384, 128], P('frame', 'orient'), may hold values from 0.5 to 2
Outputs:
- new_log_tomograms: bfloat16 [2048, 4096], P('orient', 'frame')
- volume: float32 [2, 384, 128], P('frame', 'orient')
- evidence: float32 [512], P('frame')
The draws below stay inside these ranges and needn't reach their ends.
Inputs may be any that keep to these rules, and one draw needn't show every extreme that they name: `frames`: each frame's counts lie below a level of that frame; the first frame has a pixel with 15 photons. `tile_index`: the tile of an entry counts within the shell group of its pixel block.
All inputs are finite; a program needn't handle non-finite values.
Results may differ from the reference program's by a relative error of at most 0.008.
Values may be sent and summed in bfloat16 or wider, within the bound.
A program may use at most 64 MiB of HBM per device.

```python
import math
import jax
import jax.numpy as jnp
from jax import lax

PIX = 4096
TILE = 128
ROT_DEV = 128
FR_DEV = 256
TILE_DEV = 24
ORIENTS = 2048
FRAMES = 512
BLOCKS = 32
GROUPS = 2
TILES_COL = 384
N_ORIENT = 16
N_FRAME = 2


def frame_counts(key):
    level_key, count_key = jax.random.split(jax.random.fold_in(key, 11))
    levels = jax.random.randint(level_key, (FRAMES, 1), 1, 17)
    first_frame = jnp.arange(FRAMES)[:, None] == 0
    levels = jnp.where(first_frame, 16, levels)
    raw_bits = jax.random.randint(count_key, (FRAMES, PIX), 0, 1 << 20)
    counts = raw_bits % levels
    corner = first_frame & (jnp.arange(PIX)[None, :] == 0)
    counts = jnp.where(corner, 15, counts)
    return counts.astype(jnp.int32)


def draw_frames(key, part):
    return frame_counts(key)


def draw_log_tomograms(key, part):
    base_field = 0.5 * jax.random.normal(jax.random.fold_in(key, 23), (ORIENTS, PIX), jnp.float32)
    base_field = jnp.clip(base_field, -3.0, 3.0)
    return base_field.astype(jnp.bfloat16)


def touch_ends(values, stream_key, smallest, largest):
    longest = values.shape.index(max(values.shape))
    spots = []
    for shift in (0, 1):
        where = [jax.random.randint(jax.random.fold_in(stream_key, axis), (), 0, length) for axis, length in enumerate(values.shape)]
        where[longest] = (where[longest] + shift) % values.shape[longest]
        spots.append(tuple(where))
    return values.at[spots[0]].set(smallest).at[spots[1]].set(largest)


def block_scale(rng, dims, cuts, low, top_value):
    factor_of, own = 1.0, jax.random.fold_in(rng, 6)
    for dim, parts in cuts:
        steps = jnp.exp(jax.random.uniform(jax.random.fold_in(own, dim), (parts,), jnp.float32, low / len(cuts), top_value / len(cuts)))
        factor_of = factor_of * jnp.repeat(steps, dims[dim] // parts).reshape([-1 if axis == dim else 1 for axis in range(len(dims))])
    return factor_of


def setup_inputs(seed: int = 0) -> dict:
    keys = jax.random.split(jax.random.key(seed), 6)
    log_tomograms = draw_log_tomograms(jax.random.fold_in(keys[5], 71), 0)
    frames = draw_frames(jax.random.fold_in(keys[5], 71), 0)
    tile_index = touch_ends(jax.random.randint(keys[2], (2, BLOCKS, ORIENTS), 0, TILES_COL), jax.random.fold_in(keys[2], 1), 0, TILES_COL - 1).astype(jnp.int32)
    tile_weight = jnp.clip(jnp.exp(math.log(1.0) - 2.3025851 * jax.random.uniform(keys[3], (2, BLOCKS, ORIENTS), jnp.float32) ** block_scale(keys[3], (2, BLOCKS, ORIENTS), ((1, 2), (2, 16)), -0.2, 0.2)), 0.1, 1.0)
    prior_volume = jnp.clip(jnp.exp(math.log(2.0) - 1.3862944 * jax.random.uniform(keys[4], (GROUPS, TILES_COL, TILE), jnp.float32) ** block_scale(keys[4], (GROUPS, TILES_COL, TILE), ((0, 2), (1, 16)), -0.2, 0.2)), 0.5, 2.0)
    return {"log_tomograms": log_tomograms, "frames": frames, "tile_index": tile_index, "tile_weight": tile_weight, "prior_volume": prior_volume}


def reference(log_tomograms, frames, tile_index, tile_weight, prior_volume):
    inverse_temp = 64.0 / PIX
    counts = frames.astype(jnp.bfloat16)
    intensity = jnp.exp(log_tomograms.astype(jnp.float32))
    tomo_mass = jnp.sum(intensity, axis=1)
    correlation = jnp.dot(log_tomograms, counts.T, preferred_element_type=jnp.float32)
    scores = inverse_temp * (correlation - tomo_mass[:, None])
    score_peak = jnp.max(scores, axis=0)
    shifted = jnp.exp(scores - score_peak[None, :])
    score_total = jnp.sum(shifted, axis=0)
    responsibility = shifted / score_total[None, :]
    evidence = score_peak + jnp.log(score_total)
    resp_low = responsibility.astype(jnp.bfloat16)
    prior_share = (FR_DEV * N_FRAME) / (ROT_DEV * N_ORIENT)
    group_blocks = PIX // TILE // N_FRAME
    block_count = PIX // TILE
    tiles_column = TILE_DEV * N_ORIENT
    prior_weight = ROT_DEV * group_blocks / (4.0 * TILE_DEV)
    segment_base = (jnp.arange(block_count, dtype=jnp.int32) // group_blocks) * tiles_column

    def shard_update(first_row):
        numerator = jnp.zeros((ROT_DEV, PIX), jnp.float32)
        denominator = jnp.zeros((ROT_DEV,), jnp.float32)
        for frame_group in range(N_FRAME):
            column_first = jnp.int32(frame_group * FR_DEV)
            resp_part = lax.dynamic_slice(resp_low, (first_row, column_first), (ROT_DEV, FR_DEV))
            exact_part = lax.dynamic_slice(responsibility, (first_row, column_first), (ROT_DEV, FR_DEV))
            group_counts = counts[frame_group * FR_DEV:(frame_group + 1) * FR_DEV]
            numer_term = jnp.dot(resp_part, group_counts, preferred_element_type=jnp.float32)
            numer_term = lax.optimization_barrier(numer_term.astype(jnp.bfloat16)).astype(jnp.float32)
            denom_term = lax.optimization_barrier(jnp.sum(exact_part, axis=1).astype(jnp.bfloat16)).astype(jnp.float32)
            numerator = numerator + numer_term
            denominator = denominator + denom_term
        own_intensity = lax.dynamic_slice_in_dim(intensity, first_row, ROT_DEV, 0)
        return (numerator + prior_share * own_intensity) / (denominator[:, None] + prior_share)

    def shard_entries(first_row):
        shard_ids = lax.dynamic_slice_in_dim(tile_index, first_row, ROT_DEV, 2)
        shard_weight = lax.dynamic_slice_in_dim(tile_weight, first_row, ROT_DEV, 2)
        segment_ids = shard_ids + segment_base[None, :, None]
        return segment_ids, shard_weight

    def accumulate(running, shard_index):
        first_row = (shard_index * ROT_DEV).astype(jnp.int32)
        updated = shard_update(first_row)
        block_values = updated.reshape(ROT_DEV, block_count, TILE).transpose(1, 0, 2)
        segment_ids, shard_weight = shard_entries(first_row)
        contrib = shard_weight[..., None] * block_values[None]
        flat_ids = segment_ids.reshape(-1)
        numer_tiles = running[0] + jax.ops.segment_sum(contrib.reshape(-1, TILE), flat_ids, num_segments=N_FRAME * tiles_column)
        weight_tiles = running[1] + jax.ops.segment_sum(shard_weight.reshape(-1), flat_ids, num_segments=N_FRAME * tiles_column)
        return (numer_tiles, weight_tiles), None

    start_state = (jnp.zeros((N_FRAME * tiles_column, TILE), jnp.float32), jnp.zeros((N_FRAME * tiles_column,), jnp.float32))
    (numer_tiles, weight_tiles), _ = lax.scan(accumulate, start_state, jnp.arange(N_ORIENT, dtype=jnp.int32))
    prior_flat = prior_volume.reshape(N_FRAME * tiles_column, TILE)
    volume_flat = (numer_tiles + prior_weight * prior_flat) / (weight_tiles[:, None] + prior_weight)
    volume = volume_flat.reshape(N_FRAME, tiles_column, TILE)

    def slice_shard(shard_index):
        first_row = (shard_index * ROT_DEV).astype(jnp.int32)
        segment_ids, shard_weight = shard_entries(first_row)
        picked = volume_flat[segment_ids]
        blended = jnp.sum(shard_weight[..., None] * picked, axis=0) / jnp.sum(shard_weight, axis=0)[..., None]
        return jnp.log(blended).transpose(1, 0, 2).reshape(ROT_DEV, PIX).astype(jnp.bfloat16)

    new_log = lax.map(slice_shard, jnp.arange(N_ORIENT, dtype=jnp.int32)).reshape(ORIENTS, PIX)
    return (new_log, volume, evidence)
```

```python
import functools

import jax
import jax.numpy as jnp
from jax import lax
from jax.experimental import pallas as pl
from jax.experimental.pallas import tpu as pltpu
from jax.sharding import PartitionSpec as P

MESH = pl.DeviceIdType.MESH
F32 = jnp.float32
BF16 = jnp.bfloat16
GROUP = 8
CHUNKS = 4
OWN = 2


def remote(src, dst, send_sem, recv_sem, where):
    return pltpu.make_async_remote_copy(
        src_ref=src,
        dst_ref=dst,
        send_sem=send_sem,
        recv_sem=recv_sem,
        device_id=where,
        device_id_type=MESH,
    )


def far_first(count):
    return sorted(range(1, count), key=lambda d: -min(d, count - d))


def each(order, body):
    if len(order) <= 32:
        for d in order:
            body(d)
    else:

        def step(d, carry):
            body(d)
            return carry

        lax.fori_loop(1, len(order) + 1, step, 0)


def kernel(
    n_orient,
    n_frame,
    logt_hbm,
    frames_hbm,
    index_hbm,
    weight_hbm,
    prior_hbm,
    new_log_ref,
    volume_ref,
    evidence_ref,
    logt,
    frames,
    index_ref,
    weight_ref,
    prior_ref,
    away,
    pool,
    intensity,
    share_all,
    stat_all,
    resp_all,
    spread,
    update,
    sums,
    sums_in,
    gathered,
    tile_out,
    tile_in,
    tiles,
    tiles_t,
    in_sem,
    hello,
    count_send,
    count_recv,
    share_send,
    share_recv,
    fan_send,
    fan_recv,
):
    me = lax.axis_index("orient")
    mine = lax.axis_index("frame")
    rot_rows = logt.shape[1]
    frame_rows = frames.shape[1]
    group_blocks = index_ref.shape[1]
    tile_rows, width = prior_ref.shape[1:]
    columns = logt.shape[2]
    pixels = columns * n_frame
    tile_count = tile_rows * n_orient
    chunk = (384 // tile_rows if n_orient % max(384 // tile_rows, 1) == 0 else 1) * tile_rows
    piece = frame_rows // GROUP
    hop = columns // CHUNKS

    place_in = lax.rem(me, GROUP)
    base = me - place_in
    core = lax.rem(place_in, 2)
    low = lax.rem(place_in // 2, 2)
    high = place_in // 4
    parity = lax.rem(low + high, 2)
    partner = me + 1 - 2 * core
    beside = me + 2 - 4 * low
    above = me + 4 - 8 * high

    barrier = pltpu.get_barrier_semaphore()

    def signal(sem, where):
        pl.semaphore_signal(sem, inc=1, device_id=where, device_id_type=MESH)

    groups = n_orient // GROUP

    def greet_group(sem):
        for i in range(1, GROUP):
            signal(sem, {"orient": base + lax.rem(place_in + i, GROUP)})

    def greet_frames(sem):
        for d in range(1, n_frame):
            signal(sem, {"frame": lax.rem(mine + d, n_frame)})

    greet_frames(barrier)
    greet_group(barrier)
    each(
        list(range(1, groups)),
        lambda k: signal(barrier, {"orient": lax.rem(me + k * GROUP, n_orient)}),
    )

    def rows_of(quarter):
        return pl.ds(pl.multiple_of(quarter * 2 * piece, 2 * piece), 2 * piece)

    def columns_of(d):
        return pl.ds(pl.multiple_of(lax.rem(mine + d, n_frame) * columns, 128), columns)

    my_quarter = parity * 2 + core

    def load(source, target, sem):
        copy = pltpu.make_async_copy(source, target, sem)
        copy.start()
        return copy

    first_copies = [
        load(
            frames_hbm.at[rows_of(my_quarter), columns_of(d)],
            frames.at[d, rows_of(my_quarter)],
            in_sem.at[0, d],
        )
        for d in range(1, n_frame)
    ]
    logt_copies = {}
    rest_copies = {}
    for d in range(1, n_frame):
        logt_copies[d] = load(logt_hbm.at[:, columns_of(d)], logt.at[d], in_sem.at[1, d])
        for i in range(1, 4):
            rows = rows_of(lax.rem(my_quarter + i, 4))
            load(frames_hbm.at[rows, columns_of(d)], frames.at[d, rows], in_sem.at[2, d])
        rest = frames.at[d, pl.ds(0, 6 * piece)]
        rest_copies[d] = pltpu.make_async_copy(rest, rest, in_sem.at[2, d])
    logt_copies[0] = load(logt_hbm.at[:, columns_of(0)], logt.at[0], in_sem.at[0, 0])
    own_copies = []
    own = columns // OWN
    for c in range(OWN):
        cols = pl.ds(pl.multiple_of(mine * columns + c * own, 128), own)
        own_copies.append(
            load(
                frames_hbm.at[:, cols],
                frames.at[0, :, pl.ds(c * own, own)],
                in_sem.at[1 + c, 0],
            )
        )
    small_copies = [
        load(source, target, in_sem.at[3, i])
        for i, (source, target) in enumerate(((index_hbm, index_ref), (weight_hbm, weight_ref)))
    ]
    small_copies.append(load(prior_hbm, prior_ref, in_sem.at[4, 0]))

    for d in range(1, n_frame):
        first_copies[d - 1].wait()
        away[d - 1, rows_of(my_quarter)] = frames[d, rows_of(my_quarter)].astype(F32).astype(BF16)

    pl.semaphore_wait(barrier, GROUP - 1 + groups - 1 + n_frame - 1)

    def part_rows(side, kind):
        return pl.ds(
            pl.multiple_of((side * 4 + core * 2 + kind) * piece, piece), piece
        )

    def part_cols(k, start=0):
        return pl.ds(pl.multiple_of(start + k * hop, 128), hop)

    def source_of(d):
        return lax.rem(mine + n_frame - d, n_frame)

    relayed = part_rows(parity, low)
    kept = part_rows(parity, 1 - low)
    cross = {}
    for kind, rows in ((0, relayed), (1, kept)):
        for k in range(CHUNKS):
            for d in range(1, n_frame):
                cross[kind, k, d] = remote(
                    away.at[d - 1, rows, part_cols(k)],
                    pool.at[mine, rows, part_cols(k)],
                    count_send.at[0],
                    count_recv.at[kind, d - 1, k],
                    {"frame": lax.rem(mine + d, n_frame)},
                )
                cross[kind, k, d].start()
    greet_group(hello.at[0])

    onward = {}

    def send_on(kind, rows, k, d, to):
        where = pool.at[source_of(d), rows, part_cols(k)]
        onward[kind, k, d] = remote(
            where, where, count_send.at[0], count_recv.at[kind, d - 1, k], {"orient": to}
        )
        onward[kind, k, d].start()

    def relay(k):
        for d in range(1, n_frame):
            cross[0, k, d].wait_recv()
            send_on(2, relayed, k, d, beside)
            send_on(3, relayed, k, d, above)

    def pass_on(k):
        for d in range(1, n_frame):
            onward[2, k, d].wait_recv()
            onward[3, k, d].wait_recv()
            send_on(4, rows_of((1 - parity) * 2 + core), k, d, partner)
        for d in range(1, n_frame):
            cross[1, k, d].wait_recv()
            send_on(5, rows_of(my_quarter), k, d, partner)

    def arrived(k):
        for d in range(1, n_frame):
            onward[4, k, d].wait_recv()
            onward[5, k, d].wait_recv()

    mass = jnp.zeros((rot_rows, 128), F32)
    correlation = jnp.zeros((rot_rows, frame_rows), F32)
    contract = (((1,), (1,)), ((), ()))

    def exponentials(slot, mass):
        for c in range(columns // 512 if columns % 512 == 0 else 1):
            span = min(columns, 512)
            value = jnp.exp(logt[slot, :, c * span : (c + 1) * span].astype(F32))
            if slot == 0:
                intensity[:, c * span : (c + 1) * span] = value
            for k in range(span // 128):
                mass = mass + value[:, k * 128 : (k + 1) * 128]
        return mass

    for d in range(1, n_frame):
        logt_copies[d].wait()
        mass = exponentials(d, mass)
        rest_copies[d].wait()
        for i in range(1, 4):
            rows = rows_of(lax.rem(my_quarter + i, 4))
            away[d - 1, rows] = frames[d, rows].astype(F32).astype(BF16)
        correlation = correlation + lax.dot_general(
            logt[d], away[d - 1], contract, preferred_element_type=F32
        )
    logt_copies[0].wait()
    mass = exponentials(0, mass)
    for c in range(OWN):
        own_copies[c].wait()
        cols = slice(c * own, (c + 1) * own)
        low_counts = frames[0, :, cols].astype(F32).astype(BF16)
        pool[mine, :, cols] = low_counts
        correlation = correlation + lax.dot_general(
            logt[0, :, cols], low_counts, contract, preferred_element_type=F32
        )

    pl.semaphore_wait(hello.at[0], GROUP - 1)
    greet_frames(hello.at[1])

    score = (64.0 / pixels) * (correlation - jnp.sum(mass, axis=1, keepdims=True))
    peak = jnp.max(score, axis=0, keepdims=True)
    grown = jnp.exp(score - peak)
    share_all[mine] = grown.astype(BF16)
    here = mine * n_orient + me
    stat_all[here, 0:1, :] = peak
    stat_all[here, 1:2, :] = jnp.sum(grown, axis=0, keepdims=True)
    share_copies = []
    for d in range(1, n_frame):
        copy = remote(
            share_all.at[mine],
            share_all.at[mine],
            share_send.at[d - 1],
            share_recv.at[d - 1],
            {"frame": lax.rem(mine + d, n_frame)},
        )
        copy.start()
        share_copies.append(copy)
    pl.semaphore_wait(hello.at[1], n_frame - 1)

    def send_stat(d, to):
        remote(
            stat_all.at[here],
            stat_all.at[here],
            fan_send.at[0],
            fan_recv.at[0],
            {"orient": lax.rem(me + d, n_orient), "frame": to},
        ).start()

    for e in range(1, n_frame):
        to = lax.rem(mine + e, n_frame)
        each(far_first(n_orient), lambda d: send_stat(d, to))
        send_stat(0, to)
    each(far_first(n_orient), lambda d: send_stat(d, mine))

    for copy in small_copies:
        copy.wait()
    weight_low = weight_ref[...].astype(BF16).astype(F32)
    index = index_ref[...]
    lane = lax.broadcasted_iota(jnp.int32, (8, 128), 1)
    joint = spread.shape[1] // tile_rows
    strip = joint * tile_rows

    def build(o, carry):
        first = o * strip
        row_id = lax.broadcasted_iota(jnp.int32, (strip, rot_rows), 0) + first
        total = jnp.zeros((strip, rot_rows), F32)
        for j in range(group_blocks):
            value = jnp.where(row_id == index[0, j][None, :], weight_low[0, j][None, :], 0.0)
            value = value + jnp.where(
                row_id == index[1, j][None, :], weight_low[1, j][None, :], 0.0
            )
            narrow = value.astype(BF16)
            total = total + narrow.astype(F32)
            spread[o, :, j * rot_rows : (j + 1) * rot_rows] = narrow
        weight_sum = jnp.sum(total, axis=1, keepdims=True)
        for i in range(joint):
            packed = jnp.zeros((8, 128), F32)
            for b in range(tile_rows // 8):
                at = i * tile_rows + b * 8
                exact = weight_sum[at : at + 8]
                upper = exact.astype(BF16).astype(F32)
                packed = packed + jnp.where(lane == b, upper, 0.0)
                packed = packed + jnp.where(lane == 64 + b, exact - upper, 0.0)
            sums[o * joint + i] = packed.astype(BF16)
        return carry

    builds = n_orient // joint
    lax.fori_loop(0, builds // 2, build, 0)
    relay(0)
    lax.fori_loop(builds // 2, 3 * builds // 4, build, 0)
    relay(1)
    lax.fori_loop(3 * builds // 4, builds, build, 0)

    def send_sums(d):
        to = lax.rem(me + d, n_orient)
        remote(
            sums.at[to], sums_in.at[d - 1], fan_send.at[3], fan_recv.at[3], {"orient": to}
        ).start()

    for k in range(2, CHUNKS):
        relay(k)
    each(far_first(n_orient), send_sums)
    for k in range(2):
        pass_on(k)

    stats_there = stat_all.at[pl.ds(0, n_orient * n_frame - 1)]
    pltpu.make_async_copy(stats_there, stats_there, fan_recv.at[0]).wait()
    for copy in share_copies:
        copy.wait_recv()
    den_all = jnp.zeros((rot_rows, 1), F32)
    for f in range(n_frame):
        peaks = stat_all[f * n_orient : (f + 1) * n_orient, 0, :]
        totals = stat_all[f * n_orient : (f + 1) * n_orient, 1, :]
        peak = jnp.max(peaks, axis=0, keepdims=True)
        total = jnp.sum(totals * jnp.exp(peaks - peak), axis=0, keepdims=True)
        scale = jnp.exp(stat_all[f * n_orient + me, 0:1, :] - peak) / total
        resp = share_all[f].astype(F32) * scale
        resp_all[f] = resp.astype(BF16)
        den_all = den_all + jnp.sum(resp, axis=1, keepdims=True)

        @pl.when(mine == f)
        def _():
            evidence_ref[...] = peak + jnp.log(total)

    share = frame_rows * n_frame / (rot_rows * n_orient)
    inverse = 1.0 / (den_all + share)
    blocks = hop // width

    def process(k):
        cols = slice(k * hop, (k + 1) * hop)
        value = share * intensity[:, cols]
        for f in range(n_frame):
            value = value + jnp.dot(resp_all[f], pool[f, :, cols], preferred_element_type=F32)
        value = value * inverse
        for b in range(blocks):
            j = k * blocks + b
            update[j * rot_rows : (j + 1) * rot_rows] = value[
                :, b * width : (b + 1) * width
            ].astype(BF16)
        deep = slice(k * blocks * rot_rows, (k + 1) * blocks * rot_rows)

        def gather(c, carry):
            block = spread[pl.ds(c * (chunk // strip), chunk // strip), :, deep]
            summed = jnp.dot(
                block.reshape(chunk, blocks * rot_rows), update[deep], preferred_element_type=F32
            )
            if k > 0:
                summed = summed + gathered[c]
            if k < CHUNKS - 1:
                gathered[c] = summed
            else:
                for i in range(chunk // tile_rows):
                    tile_out[c * (chunk // tile_rows) + i] = summed[
                        i * tile_rows : (i + 1) * tile_rows
                    ].astype(BF16)
            return carry

        lax.fori_loop(0, tile_count // chunk, gather, 0)

    pass_on(2)
    arrived(0)
    process(0)
    pass_on(3)
    arrived(1)
    process(1)
    arrived(2)
    process(2)
    arrived(3)
    process(3)

    def send_tiles(d):
        to = lax.rem(me + d, n_orient)
        remote(
            tile_out.at[to], tile_in.at[d - 1], fan_send.at[1], fan_recv.at[1], {"orient": to}
        ).start()

    each(far_first(n_orient), send_tiles)

    prior_weight = rot_rows * group_blocks / (4.0 * tile_rows)
    pltpu.make_async_copy(sums_in, sums_in, fan_recv.at[3]).wait()
    packed = lax.fori_loop(
        0, n_orient - 1, lambda d, so_far: so_far + sums_in[d].astype(F32), sums[me].astype(F32)
    )
    weight = jnp.concatenate(
        [packed[:, b : b + 1] + packed[:, 64 + b : 65 + b] for b in range(tile_rows // 8)], axis=0
    )
    weight = 1.0 / (weight + prior_weight)
    prior = prior_weight * prior_ref[0] + tile_out[me].astype(F32)
    both = weight_low[0] + weight_low[1]
    both = jnp.where(index[0] == index[1], both.astype(BF16).astype(F32), both)
    scale = 1.0 / both

    pltpu.make_async_copy(tile_in, tile_in, fan_recv.at[1]).wait()
    whole = lax.fori_loop(
        0, n_orient - 1, lambda d, so_far: so_far + tile_in[d].astype(F32), prior
    )
    value = whole * weight
    volume_ref[0] = value
    tiles[me] = (value - 1.0).astype(BF16)

    def send_volume(d):
        where = tiles.at[me]
        remote(
            where, where, fan_send.at[2], fan_recv.at[2], {"orient": lax.rem(me + d, n_orient)}
        ).start()

    each(far_first(n_orient), send_volume)

    pltpu.make_async_copy(away, away, count_send.at[0]).wait()
    for copy in share_copies:
        copy.wait_send()
    pltpu.make_async_copy(stats_there, stats_there, fan_send.at[0]).wait()
    pltpu.make_async_copy(sums_in, sums_in, fan_send.at[3]).wait()
    pltpu.make_async_copy(tile_in, tile_in, fan_send.at[1]).wait()
    incoming = tiles.at[pl.ds(0, n_orient - 1)]
    pltpu.make_async_copy(incoming, incoming, fan_recv.at[2]).wait()
    owners = chunk // tile_rows

    def turn(c, carry):
        value = tiles[pl.ds(c * owners, owners)].astype(F32).reshape(chunk, width)
        tiles_t[:, pl.ds(pl.multiple_of(c * chunk, 128), chunk)] = value.T.astype(BF16)
        return carry

    lax.fori_loop(0, tile_count // chunk, turn, 0)
    pair = 2 if group_blocks % 2 == 0 else 1
    for c in range(group_blocks // pair):
        cols = slice(c * pair * rot_rows, (c + 1) * pair * rot_rows)
        block = spread[:, :, cols].reshape(tile_count, pair * rot_rows)
        blended = jnp.dot(tiles_t[...], block, preferred_element_type=F32)
        for k in range(pair):
            j = c * pair + k
            value = blended[:, k * rot_rows : (k + 1) * rot_rows] * scale[j][None, :]
            value = jnp.log(1.0 + value)
            new_log_ref[:, j * width : (j + 1) * width] = value.T.astype(BF16)
    pltpu.make_async_copy(incoming, incoming, fan_send.at[2]).wait()


def place(a_in, b_in, c_in, a_out, b_out, c_out, sem):
    copies = [
        pltpu.make_async_copy(source, target, sem.at[i])
        for i, (source, target) in enumerate(((a_in, a_out), (b_in, b_out), (c_in, c_out)))
    ]
    for copy in copies:
        copy.start()
    for copy in copies:
        copy.wait()


def on_device(log_tomograms, frames, tile_index, tile_weight, prior_volume):
    n_orient = lax.axis_size("orient")
    n_frame = lax.axis_size("frame")
    rot_rows, pixels = log_tomograms.shape
    frame_rows = frames.shape[0]
    group_blocks = tile_index.shape[1]
    tile_rows, width = prior_volume.shape[1:]
    columns = pixels // n_frame
    tile_count = tile_rows * n_orient
    others = max(n_frame - 1, 1)
    chunk = (384 // tile_rows if n_orient % max(384 // tile_rows, 1) == 0 else 1) * tile_rows
    dma = pltpu.SemaphoreType.DMA
    vmem = pl.BlockSpec(memory_space=pltpu.VMEM)
    hbm = pl.BlockSpec(memory_space=pltpu.HBM)
    new_log, volume, evidence = pl.pallas_call(
        functools.partial(kernel, n_orient, n_frame),
        out_shape=(
            pltpu.VMEM((rot_rows, columns), BF16),
            pltpu.VMEM((1, tile_rows, width), F32),
            pltpu.VMEM((1, frame_rows), F32),
        ),
        in_specs=[hbm] * 5,
        out_specs=(vmem, vmem, vmem),
        scratch_shapes=[
            pltpu.VMEM((n_frame, rot_rows, columns), BF16),
            pltpu.VMEM((n_frame, frame_rows, columns), jnp.int32),
            pltpu.VMEM(tile_index.shape, jnp.int32),
            pltpu.VMEM(tile_weight.shape, F32),
            pltpu.VMEM(prior_volume.shape, F32),
            pltpu.VMEM((others, frame_rows, columns), BF16),
            pltpu.VMEM((n_frame, frame_rows, columns), BF16),
            pltpu.VMEM((rot_rows, columns), F32),
            pltpu.VMEM((n_frame, rot_rows, frame_rows), BF16),
            pltpu.VMEM((n_frame * n_orient, 2, frame_rows), F32),
            pltpu.VMEM((n_frame, rot_rows, frame_rows), BF16),
            pltpu.VMEM((n_orient // 2, 2 * tile_rows, group_blocks * rot_rows), BF16),
            pltpu.VMEM((group_blocks * rot_rows, width), BF16),
            pltpu.VMEM((n_orient, 8, width), BF16),
            pltpu.VMEM((n_orient - 1, 8, width), BF16),
            pltpu.VMEM((tile_count // chunk, chunk, width), F32),
            pltpu.VMEM((n_orient, tile_rows, width), BF16),
            pltpu.VMEM((n_orient - 1, tile_rows, width), BF16),
            pltpu.VMEM((n_orient, tile_rows, width), BF16),
            pltpu.VMEM((width, tile_count), BF16),
            dma((5, max(n_frame, 2))),
            pltpu.SemaphoreType.REGULAR((2,)),
            dma((1,)),
            dma((6, others, CHUNKS)),
            dma((others,)),
            dma((others,)),
            dma((4,)),
            dma((4,)),
        ],
        compiler_params=pltpu.CompilerParams(
            collective_id=0, has_side_effects=True, vmem_limit_bytes=48 * 1024 * 1024
        ),
    )(*(
        pltpu.with_memory_space_constraint(value, pltpu.HBM)
        for value in (log_tomograms, frames, tile_index, tile_weight, prior_volume)
    ))
    made = (new_log, volume, evidence)
    new_log, volume, evidence = pl.pallas_call(
        place,
        out_shape=tuple(jax.ShapeDtypeStruct(value.shape, value.dtype) for value in made),
        in_specs=[vmem] * 3,
        out_specs=(hbm,) * 3,
        scratch_shapes=[dma((3,))],
        compiler_params=pltpu.CompilerParams(vmem_limit_bytes=4 * 1024 * 1024),
    )(*made)
    return (new_log, volume, evidence.reshape(frame_rows))


def solution(mesh):
    placed = (
        P("orient", None),
        P("frame", None),
        P(None, "frame", "orient"),
        P(None, "frame", "orient"),
        P("frame", "orient", None),
    )
    return jax.shard_map(
        on_device,
        mesh=mesh,
        in_specs=placed,
        out_specs=(P("orient", "frame"), P("frame", "orient", None), P("frame")),
        check_vma=False,
    )
```

```python
import functools

import jax
import jax.numpy as jnp
from jax import lax
from jax.experimental import pallas as pl
from jax.experimental.pallas import tpu as pltpu
from jax.sharding import PartitionSpec as P

MESH = pl.DeviceIdType.MESH
F32 = jnp.float32
BF16 = jnp.bfloat16
GROUP = 8
CHUNKS = 4


def remote(src, dst, send_sem, recv_sem, where):
    return pltpu.make_async_remote_copy(
        src_ref=src,
        dst_ref=dst,
        send_sem=send_sem,
        recv_sem=recv_sem,
        device_id=where,
        device_id_type=MESH,
    )


def far_first(count):
    return sorted(range(1, count), key=lambda d: -min(d, count - d))


def each(order, body):
    if len(order) <= 32:
        for d in order:
            body(d)
    else:

        def step(d, carry):
            body(d)
            return carry

        lax.fori_loop(1, len(order) + 1, step, 0)


def kernel(
    n_orient,
    n_frame,
    logt_hbm,
    frames_hbm,
    index_hbm,
    weight_hbm,
    prior_hbm,
    new_log_ref,
    volume_ref,
    evidence_ref,
    logt,
    logt_pair,
    frames,
    index_ref,
    index_pair,
    weight_ref,
    weight_pair,
    prior_ref,
    away,
    near,
    other,
    intensity,
    share_all,
    stat_all,
    resp_all,
    spread,
    spread_pair,
    update,
    sums,
    sums_in,
    gathered,
    tile_out,
    tile_in,
    tiles,
    tiles_t,
    in_sem,
    hello,
    count_send,
    count_recv,
    pair_send,
    pair_recv,
    share_send,
    share_recv,
    fan_send,
    fan_recv,
):
    me = lax.axis_index("orient")
    mine = lax.axis_index("frame")
    rot_rows = logt.shape[2]
    frame_rows = frames.shape[2]
    group_blocks = index_ref.shape[1]
    half_blocks = group_blocks // 2
    tile_rows, width = prior_ref.shape[1:]
    half = logt.shape[3]
    columns = 2 * half
    pixels = columns * n_frame
    tile_count = tile_rows * n_orient
    chunk = (384 // tile_rows if n_orient % max(384 // tile_rows, 1) == 0 else 1) * tile_rows
    quarter = frame_rows // 4
    hop = half // CHUNKS

    place_in = lax.rem(me, GROUP)
    base = me - place_in
    core = lax.rem(place_in, 2)
    low = lax.rem(place_in // 2, 2)
    high = place_in // 4
    parity = lax.rem(low + high, 2)
    partner = me + 1 - 2 * core
    beside = me + 2 - 4 * low
    above = me + 4 - 8 * high

    barrier = pltpu.get_barrier_semaphore()

    def signal(sem, where):
        pl.semaphore_signal(sem, inc=1, device_id=where, device_id_type=MESH)

    groups = n_orient // GROUP

    def greet_group(sem):
        for e in range(n_frame):
            for i in range(GROUP):
                if e + i > 0:
                    where = base + lax.rem(place_in + i, GROUP)
                    signal(sem, {"orient": where, "frame": lax.rem(mine + e, n_frame)})

    def greet_alike(sem):
        for e in range(n_frame):
            to = lax.rem(mine + e, n_frame)
            each(
                list(range(1, groups)),
                lambda k: signal(
                    sem, {"orient": lax.rem(me + k * GROUP, n_orient), "frame": to}
                ),
            )

    def rows_of(q, count=1):
        return pl.ds(pl.multiple_of(q * quarter, quarter), count * quarter)

    def columns_of(d, side):
        start = lax.rem(mine + d, n_frame) * columns + (core + side - 2 * core * side) * half
        return pl.ds(pl.multiple_of(start, 128), half)

    def source_of(d):
        return lax.rem(mine + n_frame - d, n_frame)

    def load(source, target, sem):
        copy = pltpu.make_async_copy(source, target, sem)
        copy.start()
        return copy

    mine_rows = rows_of(parity * 2, 2)
    rest_rows = rows_of(2 - parity * 2, 2)
    first_copies = [
        load(
            frames_hbm.at[mine_rows, columns_of(d, 0)],
            frames.at[d, 0, mine_rows],
            in_sem.at[0, d - 1],
        )
        for d in range(1, n_frame)
    ]
    greet_alike(barrier)
    greet_group(barrier)

    loads = {}
    for d in (*range(1, n_frame), 0):
        for side in range(2):
            first = load(
                logt_hbm.at[:, columns_of(d, side)], logt.at[d, side], in_sem.at[1 + side, d]
            )
            rows = rest_rows if d > 0 and side == 0 else pl.ds(0, frame_rows)
            rest = load(
                frames_hbm.at[rows, columns_of(d, side)],
                frames.at[d, side, rows],
                in_sem.at[3 + side, d],
            )
            loads[d, side] = (first, rest)
    small_copies = [
        load(index_hbm, index_ref, in_sem.at[5, 0]),
        load(weight_hbm, weight_ref, in_sem.at[5, 1]),
        load(prior_hbm, prior_ref, in_sem.at[0, n_frame - 1]),
    ]

    for d in range(1, n_frame):
        first_copies[d - 1].wait()
        away[d - 1, mine_rows] = frames[d, 0, mine_rows].astype(F32).astype(BF16)

    pl.semaphore_wait(barrier, groups * n_frame - n_frame + GROUP * n_frame - 1)

    relayed = rows_of(parity * 2 + low)
    kept = rows_of(parity * 2 + 1 - low)
    cross = {}

    def part_cols(k):
        return pl.ds(k * hop, hop)

    def send_across(kind, rows):
        for k in range(CHUNKS):
            for d in range(1, n_frame):
                cross[kind, k, d] = remote(
                    away.at[d - 1, rows, part_cols(k)],
                    other.at[d - 1, rows, part_cols(k)],
                    count_send.at[0],
                    count_recv.at[kind, d - 1, k],
                    {"frame": lax.rem(mine + d, n_frame)},
                )
                cross[kind, k, d].start()

    greet_group(hello.at[0])
    send_across(0, relayed)

    def relay(k):
        for d in range(1, n_frame):
            cross[0, k, d].wait_recv()
            where = other.at[d - 1, relayed, part_cols(k)]
            for to in (beside, above):
                remote(
                    where, where, count_send.at[0], count_recv.at[2, d - 1, k], {"orient": to}
                ).start()

    def arrived(k):
        for d in range(1, n_frame):
            where = other.at[d - 1, rest_rows, part_cols(k)]
            pltpu.make_async_copy(where, where, count_recv.at[2, d - 1, k]).wait()
            cross[1, k, d].wait_recv()

    mass = jnp.zeros((rot_rows, 128), F32)
    correlation = jnp.zeros((rot_rows, frame_rows), F32)
    contract = (((1,), (1,)), ((), ()))

    for d in (*range(1, n_frame), 0):
        for side in range(2):
            loads[d, side][0].wait()
            value = jnp.exp(logt[d, side].astype(F32))
            if d == 0 and side == 0:
                intensity[0] = value
            for k in range(half // 128):
                mass = mass + value[:, k * 128 : (k + 1) * 128]
            loads[d, side][1].wait()
            if d > 0 and side == 0:
                away[d - 1, rest_rows] = frames[d, 0, rest_rows].astype(F32).astype(BF16)
                counts = away[d - 1]
            else:
                counts = frames[d, side].astype(F32).astype(BF16)
                if d == 0 and side == 0:
                    near[...] = counts
            correlation = correlation + lax.dot_general(
                logt[d, side], counts, contract, preferred_element_type=F32
            )

    score = (64.0 / pixels) * (correlation - jnp.sum(mass, axis=1, keepdims=True))
    peak = jnp.max(score, axis=0, keepdims=True)
    grown = jnp.exp(score - peak)
    share_all[0, 0] = grown.astype(BF16)
    here = mine * n_orient + me
    stat_all[here, 0:1, :] = peak
    stat_all[here, 1:2, :] = jnp.sum(grown, axis=0, keepdims=True)
    pl.semaphore_wait(hello.at[0], GROUP * n_frame - 1)

    def send_stat(d, to):
        remote(
            stat_all.at[here],
            stat_all.at[here],
            fan_send.at[0],
            fan_recv.at[0],
            {"orient": lax.rem(me + d, n_orient), "frame": to},
        ).start()

    for e in range(1, n_frame):
        to = lax.rem(mine + e, n_frame)
        each(far_first(n_orient), lambda d: send_stat(d, to))
        send_stat(0, to)
    each(far_first(n_orient), lambda d: send_stat(d, mine))

    def send_share(d, side, to):
        copy = remote(
            share_all.at[0 if side == 0 or d == 0 else d, 0],
            share_all.at[d, side],
            share_send.at[d, side],
            share_recv.at[d, side],
            to,
        )
        copy.start()
        return copy

    shares = {
        (d, 0): send_share(d, 0, {"frame": lax.rem(mine + d, n_frame)})
        for d in range(1, n_frame)
    }
    shares[0, 1] = send_share(0, 1, {"orient": partner})
    send_across(1, kept)
    for copy in small_copies:
        copy.wait()
    pair_copies = []
    for i, (source, target) in enumerate(
        ((index_ref, index_pair), (weight_ref, weight_pair), (logt.at[0, 1], logt_pair))
    ):
        copy = remote(source, target, pair_send.at[i], pair_recv.at[i], {"orient": partner})
        copy.start()
        pair_copies.append(copy)

    def swap(value):
        turned = jnp.concatenate([value[:, half_blocks:], value[:, :half_blocks]], axis=1)
        return jnp.where(core == 0, value, turned)

    index = swap(index_ref[...])
    weight_low = swap(weight_ref[...].astype(BF16).astype(F32))
    lane = lax.broadcasted_iota(jnp.int32, (8, 128), 1)
    joint = spread.shape[1] // tile_rows
    strip = joint * tile_rows

    def hits(row_id, index, weight, j):
        value = jnp.where(row_id == index[0, j][None, :], weight[0, j][None, :], 0.0)
        value = value + jnp.where(row_id == index[1, j][None, :], weight[1, j][None, :], 0.0)
        return value.astype(BF16)

    def build(o, carry):
        row_id = lax.broadcasted_iota(jnp.int32, (strip, rot_rows), 0) + o * strip
        total = jnp.zeros((strip, rot_rows), F32)
        for j in range(group_blocks):
            narrow = hits(row_id, index, weight_low, j)
            total = total + narrow.astype(F32)
            spread[o, :, j * rot_rows : (j + 1) * rot_rows] = narrow
        weight_sum = jnp.sum(total, axis=1, keepdims=True)
        for i in range(joint):
            packed = jnp.zeros((8, 128), F32)
            for b in range(tile_rows // 8):
                at = i * tile_rows + b * 8
                exact = weight_sum[at : at + 8]
                upper = exact.astype(BF16).astype(F32)
                packed = packed + jnp.where(lane == b, upper, 0.0)
                packed = packed + jnp.where(lane == 64 + b, exact - upper, 0.0)
            sums[o * joint + i] = packed.astype(BF16)
        return carry

    builds = n_orient // joint
    for k in range(CHUNKS):
        lax.fori_loop(k * builds // CHUNKS, (k + 1) * builds // CHUNKS, build, 0)
        relay(k)

    def send_sums(d):
        to = lax.rem(me + d, n_orient)
        remote(
            sums.at[to], sums_in.at[d - 1], fan_send.at[3], fan_recv.at[3], {"orient": to}
        ).start()

    each(far_first(n_orient), send_sums)

    for copy in pair_copies:
        copy.wait_recv()
    index_two = jnp.where(core == 0, index_pair[:, :half_blocks], index_pair[:, half_blocks:])
    weight_two = jnp.where(core == 0, weight_pair[:, :half_blocks], weight_pair[:, half_blocks:])
    weight_two = weight_two.astype(BF16).astype(F32)
    intensity[1] = jnp.exp(logt_pair[...].astype(F32))

    def build_pair(o, carry):
        row_id = lax.broadcasted_iota(jnp.int32, (strip, rot_rows), 0) + o * strip
        for j in range(half_blocks):
            spread_pair[o, :, j * rot_rows : (j + 1) * rot_rows] = hits(
                row_id, index_two, weight_two, j
            )
        return carry

    lax.fori_loop(0, builds, build_pair, 0)

    for d in range(1, n_frame):
        shares[d, 0].wait_recv()
        shares[d, 1] = send_share(d, 1, {"orient": partner})

    stats_there = stat_all.at[pl.ds(0, n_orient * n_frame - 1)]
    pltpu.make_async_copy(stats_there, stats_there, fan_recv.at[0]).wait()
    shares[0, 1].wait_recv()
    den = [jnp.zeros((rot_rows, 1), F32) for _ in range(2)]
    for d in range(n_frame):
        at = source_of(d) * n_orient
        peaks = stat_all[pl.ds(at, n_orient), 0, :]
        totals = stat_all[pl.ds(at, n_orient), 1, :]
        peak = jnp.max(peaks, axis=0, keepdims=True)
        total = jnp.sum(totals * jnp.exp(peaks - peak), axis=0, keepdims=True)
        if d == 0:
            evidence_ref[...] = peak + jnp.log(total)
        for side, owner in enumerate((me, partner)):
            if d > 0 and side == 1:
                shares[d, 1].wait_recv()
            scale = jnp.exp(stat_all[at + owner, 0:1, :] - peak) / total
            resp = share_all[d, side].astype(F32) * scale
            resp_all[d, side * rot_rows : (side + 1) * rot_rows] = resp.astype(BF16)
            den[side] = den[side] + jnp.sum(resp, axis=1, keepdims=True)

    share = frame_rows * n_frame / (rot_rows * n_orient)
    inverse = [1.0 / (value + share) for value in den]
    blocks = hop // width

    def process(k):
        cols = slice(k * hop, (k + 1) * hop)
        mixed = jnp.dot(resp_all[0], near[:, cols], preferred_element_type=F32)
        for d in range(1, n_frame):
            mixed = mixed + jnp.dot(resp_all[d], other[d - 1, :, cols], preferred_element_type=F32)
        for side in range(2):
            value = mixed[side * rot_rows : (side + 1) * rot_rows] + share * intensity[side, :, cols]
            value = value * inverse[side]
            for b in range(blocks):
                j = k * blocks + b
                update[side, j * rot_rows : (j + 1) * rot_rows] = value[
                    :, b * width : (b + 1) * width
                ].astype(BF16)
        deep = slice(k * blocks * rot_rows, (k + 1) * blocks * rot_rows)

        def gather(c, carry):
            strips = pl.ds(c * (chunk // strip), chunk // strip)
            summed = jnp.dot(
                spread[strips, :, deep].reshape(chunk, blocks * rot_rows),
                update[0, deep],
                preferred_element_type=F32,
            )
            summed = summed + jnp.dot(
                spread_pair[strips, :, deep].reshape(chunk, blocks * rot_rows),
                update[1, deep],
                preferred_element_type=F32,
            )
            if k > 0:
                summed = summed + gathered[c]
            if k < CHUNKS - 1:
                gathered[c] = summed
            else:
                for i in range(chunk // tile_rows):
                    tile_out[c * (chunk // tile_rows) + i] = summed[
                        i * tile_rows : (i + 1) * tile_rows
                    ].astype(BF16)
            return carry

        lax.fori_loop(0, tile_count // chunk, gather, 0)

    for k in range(CHUNKS):
        arrived(k)
        process(k)

    def send_tiles(d):
        to = lax.rem(me + d, n_orient)
        remote(
            tile_out.at[to], tile_in.at[d - 1], fan_send.at[1], fan_recv.at[1], {"orient": to}
        ).start()

    each(far_first(n_orient), send_tiles)

    prior_weight = rot_rows * group_blocks / (4.0 * tile_rows)
    pltpu.make_async_copy(sums_in, sums_in, fan_recv.at[3]).wait()
    packed = lax.fori_loop(
        0, n_orient - 1, lambda d, so_far: so_far + sums_in[d].astype(F32), sums[me].astype(F32)
    )
    weight = jnp.concatenate(
        [packed[:, b : b + 1] + packed[:, 64 + b : 65 + b] for b in range(tile_rows // 8)], axis=0
    )
    weight = 1.0 / (weight + prior_weight)
    prior = prior_weight * prior_ref[0] + tile_out[me].astype(F32)
    both = weight_low[0] + weight_low[1]
    both = jnp.where(index[0] == index[1], both.astype(BF16).astype(F32), both)
    scale = 1.0 / both
    for copy in pair_copies:
        copy.wait_send()
    pltpu.make_async_copy(other, other, count_send.at[0]).wait()
    for copy in shares.values():
        copy.wait_send()
    pltpu.make_async_copy(stats_there, stats_there, fan_send.at[0]).wait()
    pltpu.make_async_copy(sums_in, sums_in, fan_send.at[3]).wait()

    pltpu.make_async_copy(tile_in, tile_in, fan_recv.at[1]).wait()
    whole = lax.fori_loop(
        0, n_orient - 1, lambda d, so_far: so_far + tile_in[d].astype(F32), prior
    )
    value = whole * weight
    volume_ref[0] = value
    tiles[me] = (value - 1.0).astype(BF16)

    def send_volume(d):
        where = tiles.at[me]
        remote(
            where, where, fan_send.at[2], fan_recv.at[2], {"orient": lax.rem(me + d, n_orient)}
        ).start()

    each(far_first(n_orient), send_volume)

    pltpu.make_async_copy(tile_in, tile_in, fan_send.at[1]).wait()
    incoming = tiles.at[pl.ds(0, n_orient - 1)]
    pltpu.make_async_copy(incoming, incoming, fan_recv.at[2]).wait()
    owners = chunk // tile_rows

    def turn(c, carry):
        value = tiles[pl.ds(c * owners, owners)].astype(F32).reshape(chunk, width)
        tiles_t[:, pl.ds(pl.multiple_of(c * chunk, 128), chunk)] = value.T.astype(BF16)
        return carry

    lax.fori_loop(0, tile_count // chunk, turn, 0)
    pair = 2 if half_blocks % 2 == 0 else 1
    for c in range(group_blocks // pair):
        cols = slice(c * pair * rot_rows, (c + 1) * pair * rot_rows)
        block = spread[:, :, cols].reshape(tile_count, pair * rot_rows)
        blended = jnp.dot(tiles_t[...], block, preferred_element_type=F32)
        for k in range(pair):
            j = c * pair + k
            value = blended[:, k * rot_rows : (k + 1) * rot_rows] * scale[j][None, :]
            value = jnp.log(1.0 + value)
            where = lax.rem(core * half_blocks + j, group_blocks) * width
            new_log_ref[:, pl.ds(pl.multiple_of(where, 128), width)] = value.T.astype(BF16)
    pltpu.make_async_copy(incoming, incoming, fan_send.at[2]).wait()


def place(a_in, b_in, c_in, a_out, b_out, c_out, sem):
    copies = [
        pltpu.make_async_copy(source, target, sem.at[i])
        for i, (source, target) in enumerate(((a_in, a_out), (b_in, b_out), (c_in, c_out)))
    ]
    for copy in copies:
        copy.start()
    for copy in copies:
        copy.wait()


def on_device(log_tomograms, frames, tile_index, tile_weight, prior_volume):
    n_orient = lax.axis_size("orient")
    n_frame = lax.axis_size("frame")
    rot_rows, pixels = log_tomograms.shape
    frame_rows = frames.shape[0]
    group_blocks = tile_index.shape[1]
    tile_rows, width = prior_volume.shape[1:]
    columns = pixels // n_frame
    tile_count = tile_rows * n_orient
    others = max(n_frame - 1, 1)
    half = columns // 2
    chunk = (384 // tile_rows if n_orient % max(384 // tile_rows, 1) == 0 else 1) * tile_rows
    dma = pltpu.SemaphoreType.DMA
    vmem = pl.BlockSpec(memory_space=pltpu.VMEM)
    hbm = pl.BlockSpec(memory_space=pltpu.HBM)
    new_log, volume, evidence = pl.pallas_call(
        functools.partial(kernel, n_orient, n_frame),
        out_shape=(
            pltpu.VMEM((rot_rows, columns), BF16),
            pltpu.VMEM((1, tile_rows, width), F32),
            pltpu.VMEM((1, frame_rows), F32),
        ),
        in_specs=[hbm] * 5,
        out_specs=(vmem, vmem, vmem),
        scratch_shapes=[
            pltpu.VMEM((n_frame, 2, rot_rows, half), BF16),
            pltpu.VMEM((rot_rows, half), BF16),
            pltpu.VMEM((n_frame, 2, frame_rows, half), jnp.int32),
            pltpu.VMEM(tile_index.shape, jnp.int32),
            pltpu.VMEM(tile_index.shape, jnp.int32),
            pltpu.VMEM(tile_weight.shape, F32),
            pltpu.VMEM(tile_weight.shape, F32),
            pltpu.VMEM(prior_volume.shape, F32),
            pltpu.VMEM((others, frame_rows, half), BF16),
            pltpu.VMEM((frame_rows, half), BF16),
            pltpu.VMEM((others, frame_rows, half), BF16),
            pltpu.VMEM((2, rot_rows, half), F32),
            pltpu.VMEM((n_frame, 2, rot_rows, frame_rows), BF16),
            pltpu.VMEM((n_frame * n_orient, 2, frame_rows), F32),
            pltpu.VMEM((n_frame, 2 * rot_rows, frame_rows), BF16),
            pltpu.VMEM((n_orient // 2, 2 * tile_rows, group_blocks * rot_rows), BF16),
            pltpu.VMEM((n_orient // 2, 2 * tile_rows, group_blocks // 2 * rot_rows), BF16),
            pltpu.VMEM((2, group_blocks // 2 * rot_rows, width), BF16),
            pltpu.VMEM((n_orient, 8, width), BF16),
            pltpu.VMEM((n_orient - 1, 8, width), BF16),
            pltpu.VMEM((tile_count // chunk, chunk, width), F32),
            pltpu.VMEM((n_orient, tile_rows, width), BF16),
            pltpu.VMEM((n_orient - 1, tile_rows, width), BF16),
            pltpu.VMEM((n_orient, tile_rows, width), BF16),
            pltpu.VMEM((width, tile_count), BF16),
            dma((6, max(n_frame, 2))),
            pltpu.SemaphoreType.REGULAR((1,)),
            dma((1,)),
            dma((3, others, CHUNKS)),
            dma((3,)),
            dma((3,)),
            dma((n_frame, 2)),
            dma((n_frame, 2)),
            dma((4,)),
            dma((4,)),
        ],
        compiler_params=pltpu.CompilerParams(
            collective_id=0, has_side_effects=True, vmem_limit_bytes=48 * 1024 * 1024
        ),
    )(*(
        pltpu.with_memory_space_constraint(value, pltpu.HBM)
        for value in (log_tomograms, frames, tile_index, tile_weight, prior_volume)
    ))
    made = (new_log, volume, evidence)
    new_log, volume, evidence = pl.pallas_call(
        place,
        out_shape=tuple(jax.ShapeDtypeStruct(value.shape, value.dtype) for value in made),
        in_specs=[vmem] * 3,
        out_specs=(hbm,) * 3,
        scratch_shapes=[dma((3,))],
        compiler_params=pltpu.CompilerParams(vmem_limit_bytes=4 * 1024 * 1024),
    )(*made)
    return (new_log, volume, evidence.reshape(frame_rows))


def solution(mesh):
    placed = (
        P("orient", None),
        P("frame", None),
        P(None, "frame", "orient"),
        P(None, "frame", "orient"),
        P("frame", "orient", None),
    )
    return jax.shard_map(
        on_device,
        mesh=mesh,
        in_specs=placed,
        out_specs=(P("orient", "frame"), P("frame", "orient", None), P("frame")),
        check_vma=False,
    )
```

```python
import functools

import jax
import jax.numpy as jnp
from jax import lax
from jax.experimental import pallas as pl
from jax.experimental.pallas import tpu as pltpu
from jax.sharding import PartitionSpec as P

MESH = pl.DeviceIdType.MESH
F32 = jnp.float32
BF16 = jnp.bfloat16
GROUP = 8
CHUNKS = 2


def remote(src, dst, send_sem, recv_sem, where):
    return pltpu.make_async_remote_copy(
        src_ref=src,
        dst_ref=dst,
        send_sem=send_sem,
        recv_sem=recv_sem,
        device_id=where,
        device_id_type=MESH,
    )


def far_first(count):
    return sorted(range(1, count), key=lambda d: -min(d, count - d))


def each(order, body):
    if len(order) <= 32:
        for d in order:
            body(d)
    else:

        def step(d, carry):
            body(d)
            return carry

        lax.fori_loop(1, len(order) + 1, step, 0)


def kernel(
    n_orient,
    n_frame,
    logt_hbm,
    frames_hbm,
    index_hbm,
    weight_hbm,
    prior_hbm,
    new_log_ref,
    volume_ref,
    evidence_ref,
    logt,
    logt_pair,
    frames,
    index_ref,
    index_pair,
    weight_ref,
    weight_pair,
    prior_ref,
    away,
    near,
    other,
    intensity,
    share_all,
    stat_all,
    resp_all,
    spread,
    spread_pair,
    update,
    sums,
    sums_in,
    gathered,
    tile_out,
    tile_in,
    tiles,
    tiles_t,
    in_sem,
    hello,
    count_send,
    count_recv,
    pair_send,
    pair_recv,
    share_send,
    share_recv,
    fan_send,
    fan_recv,
):
    me = lax.axis_index("orient")
    mine = lax.axis_index("frame")
    rot_rows = logt.shape[2]
    frame_rows = frames.shape[2]
    group_blocks = index_ref.shape[1]
    half_blocks = group_blocks // 2
    tile_rows, width = prior_ref.shape[1:]
    half = logt.shape[3]
    columns = 2 * half
    pixels = columns * n_frame
    tile_count = tile_rows * n_orient
    chunk = (384 // tile_rows if n_orient % max(384 // tile_rows, 1) == 0 else 1) * tile_rows
    quarter = frame_rows // 4
    hop = half // CHUNKS

    place_in = lax.rem(me, GROUP)
    base = me - place_in
    core = lax.rem(place_in, 2)
    low = lax.rem(place_in // 2, 2)
    high = place_in // 4
    parity = lax.rem(low + high, 2)
    partner = me + 1 - 2 * core
    beside = me + 2 - 4 * low
    above = me + 4 - 8 * high

    barrier = pltpu.get_barrier_semaphore()

    def signal(sem, where):
        pl.semaphore_signal(sem, inc=1, device_id=where, device_id_type=MESH)

    groups = n_orient // GROUP

    def greet_group(sem):
        for e in range(n_frame):
            for i in range(GROUP):
                if e + i > 0:
                    where = base + lax.rem(place_in + i, GROUP)
                    signal(sem, {"orient": where, "frame": lax.rem(mine + e, n_frame)})

    def greet_alike(sem):
        for e in range(n_frame):
            to = lax.rem(mine + e, n_frame)
            each(
                list(range(1, groups)),
                lambda k: signal(
                    sem, {"orient": lax.rem(me + k * GROUP, n_orient), "frame": to}
                ),
            )

    def rows_of(q, count=1):
        return pl.ds(pl.multiple_of(q * quarter, quarter), count * quarter)

    def columns_of(d, side):
        start = lax.rem(mine + d, n_frame) * columns + (core + side - 2 * core * side) * half
        return pl.ds(pl.multiple_of(start, 128), half)

    def source_of(d):
        return lax.rem(mine + n_frame - d, n_frame)

    def load(source, target, sem):
        copy = pltpu.make_async_copy(source, target, sem)
        copy.start()
        return copy

    mine_rows = rows_of(parity * 2, 2)
    rest_rows = rows_of(2 - parity * 2, 2)
    first_copies = [
        load(
            frames_hbm.at[mine_rows, columns_of(d, 0)],
            frames.at[d, 0, mine_rows],
            in_sem.at[0, d - 1],
        )
        for d in range(1, n_frame)
    ]
    greet_alike(barrier)
    greet_group(barrier)

    loads = {}
    for d in (*range(1, n_frame), 0):
        for side in range(2):
            first = load(
                logt_hbm.at[:, columns_of(d, side)], logt.at[d, side], in_sem.at[1 + side, d]
            )
            rows = rest_rows if d > 0 and side == 0 else pl.ds(0, frame_rows)
            rest = load(
                frames_hbm.at[rows, columns_of(d, side)],
                frames.at[d, side, rows],
                in_sem.at[3 + side, d],
            )
            loads[d, side] = (first, rest)
    small_copies = [
        load(index_hbm, index_ref, in_sem.at[5, 0]),
        load(weight_hbm, weight_ref, in_sem.at[5, 1]),
        load(prior_hbm, prior_ref, in_sem.at[0, n_frame - 1]),
    ]

    for d in range(1, n_frame):
        first_copies[d - 1].wait()
        away[d - 1, mine_rows] = frames[d, 0, mine_rows].astype(F32).astype(BF16)

    pl.semaphore_wait(barrier, groups * n_frame - n_frame + GROUP * n_frame - 1)

    relayed = rows_of(parity * 2 + low)
    kept = rows_of(parity * 2 + 1 - low)
    cross = {}

    def part_cols(k):
        return pl.ds(k * hop, hop)

    def send_across(kind, rows):
        for k in range(CHUNKS):
            for d in range(1, n_frame):
                cross[kind, k, d] = remote(
                    away.at[d - 1, rows, part_cols(k)],
                    other.at[d - 1, rows, part_cols(k)],
                    count_send.at[0],
                    count_recv.at[kind, d - 1, k],
                    {"frame": lax.rem(mine + d, n_frame)},
                )
                cross[kind, k, d].start()

    greet_group(hello.at[0])
    send_across(0, relayed)

    def relay(k):
        for d in range(1, n_frame):
            cross[0, k, d].wait_recv()
            where = other.at[d - 1, relayed, part_cols(k)]
            for to in (beside, above):
                remote(
                    where, where, count_send.at[0], count_recv.at[2, d - 1, k], {"orient": to}
                ).start()

    def arrived(k):
        for d in range(1, n_frame):
            where = other.at[d - 1, rest_rows, part_cols(k)]
            pltpu.make_async_copy(where, where, count_recv.at[2, d - 1, k]).wait()
            cross[1, k, d].wait_recv()

    mass = jnp.zeros((rot_rows, 128), F32)
    correlation = jnp.zeros((rot_rows, frame_rows), F32)
    contract = (((1,), (1,)), ((), ()))

    for d in (*range(1, n_frame), 0):
        for side in range(2):
            loads[d, side][0].wait()
            value = jnp.exp(logt[d, side].astype(F32))
            if d == 0 and side == 0:
                intensity[0] = value
            for k in range(half // 128):
                mass = mass + value[:, k * 128 : (k + 1) * 128]
            loads[d, side][1].wait()
            if d > 0 and side == 0:
                away[d - 1, rest_rows] = frames[d, 0, rest_rows].astype(F32).astype(BF16)
                counts = away[d - 1]
            else:
                counts = frames[d, side].astype(F32).astype(BF16)
                if d == 0 and side == 0:
                    near[...] = counts
            correlation = correlation + lax.dot_general(
                logt[d, side], counts, contract, preferred_element_type=F32
            )

    score = (64.0 / pixels) * (correlation - jnp.sum(mass, axis=1, keepdims=True))
    peak = jnp.max(score, axis=0, keepdims=True).astype(BF16)
    grown = jnp.exp(score - peak.astype(F32))
    share_all[0, 0] = grown.astype(BF16)
    here = mine * n_orient + me
    total = jnp.sum(grown, axis=0, keepdims=True).astype(BF16)
    stat_all[here] = jnp.concatenate([peak, total], axis=0)
    def send_share(d, side, to):
        copy = remote(
            share_all.at[0 if side == 0 or d == 0 else d, 0],
            share_all.at[d, side],
            share_send.at[d, side],
            share_recv.at[d, side],
            to,
        )
        copy.start()
        return copy

    shares = {
        (d, 0): send_share(d, 0, {"frame": lax.rem(mine + d, n_frame)})
        for d in range(1, n_frame)
    }
    shares[0, 1] = send_share(0, 1, {"orient": partner})
    pl.semaphore_wait(hello.at[0], GROUP * n_frame - 1)

    def send_stat(d, to):
        remote(
            stat_all.at[here],
            stat_all.at[here],
            fan_send.at[0],
            fan_recv.at[0],
            {"orient": lax.rem(me + d, n_orient), "frame": to},
        ).start()

    for e in range(1, n_frame):
        to = lax.rem(mine + e, n_frame)
        each(far_first(n_orient), lambda d: send_stat(d, to))
        send_stat(0, to)
    each(far_first(n_orient), lambda d: send_stat(d, mine))

    send_across(1, kept)
    for copy in small_copies:
        copy.wait()
    pair_copies = []
    for i, (source, target) in enumerate(
        ((index_ref, index_pair), (weight_ref, weight_pair), (logt.at[0, 1], logt_pair))
    ):
        copy = remote(source, target, pair_send.at[i], pair_recv.at[i], {"orient": partner})
        copy.start()
        pair_copies.append(copy)

    def swap(value):
        turned = jnp.concatenate([value[:, half_blocks:], value[:, :half_blocks]], axis=1)
        return jnp.where(core == 0, value, turned)

    index = swap(index_ref[...])
    weight_low = swap(weight_ref[...].astype(BF16).astype(F32))
    lane = lax.broadcasted_iota(jnp.int32, (8, 128), 1)
    joint = spread.shape[1] // tile_rows
    strip = joint * tile_rows

    def hits(row_id, index, weight, j):
        value = jnp.where(row_id == index[0, j][None, :], weight[0, j][None, :], 0.0)
        value = value + jnp.where(row_id == index[1, j][None, :], weight[1, j][None, :], 0.0)
        return value.astype(BF16)

    def build(o, carry):
        row_id = lax.broadcasted_iota(jnp.int32, (strip, rot_rows), 0) + o * strip
        total = jnp.zeros((strip, rot_rows), F32)
        for j in range(group_blocks):
            narrow = hits(row_id, index, weight_low, j)
            total = total + narrow.astype(F32)
            spread[o, :, j * rot_rows : (j + 1) * rot_rows] = narrow
        weight_sum = jnp.sum(total, axis=1, keepdims=True)
        for i in range(joint):
            packed = jnp.zeros((8, 128), F32)
            for b in range(tile_rows // 8):
                at = i * tile_rows + b * 8
                exact = weight_sum[at : at + 8]
                upper = exact.astype(BF16).astype(F32)
                packed = packed + jnp.where(lane == b, upper, 0.0)
                packed = packed + jnp.where(lane == 64 + b, exact - upper, 0.0)
            sums[o * joint + i] = packed.astype(BF16)
        return carry

    builds = n_orient // joint
    for k in range(CHUNKS):
        lax.fori_loop(k * builds // CHUNKS, (k + 1) * builds // CHUNKS, build, 0)
        relay(k)

    def send_sums(d):
        to = lax.rem(me + d, n_orient)
        remote(
            sums.at[to], sums_in.at[d - 1], fan_send.at[3], fan_recv.at[3], {"orient": to}
        ).start()

    each(far_first(n_orient), send_sums)

    for copy in pair_copies:
        copy.wait_recv()
    index_two = jnp.where(core == 0, index_pair[:, :half_blocks], index_pair[:, half_blocks:])
    weight_two = jnp.where(core == 0, weight_pair[:, :half_blocks], weight_pair[:, half_blocks:])
    weight_two = weight_two.astype(BF16).astype(F32)
    intensity[1] = jnp.exp(logt_pair[...].astype(F32))

    def build_pair(o, carry):
        row_id = lax.broadcasted_iota(jnp.int32, (strip, rot_rows), 0) + o * strip
        for j in range(half_blocks):
            spread_pair[o, :, j * rot_rows : (j + 1) * rot_rows] = hits(
                row_id, index_two, weight_two, j
            )
        return carry

    lax.fori_loop(0, builds, build_pair, 0)

    for d in range(1, n_frame):
        shares[d, 0].wait_recv()
        shares[d, 1] = send_share(d, 1, {"orient": partner})

    stats_there = stat_all.at[pl.ds(0, n_orient * n_frame - 1)]
    pltpu.make_async_copy(stats_there, stats_there, fan_recv.at[0]).wait()
    shares[0, 1].wait_recv()
    den = [jnp.zeros((rot_rows, 1), F32) for _ in range(2)]
    for d in range(n_frame):
        at = source_of(d) * n_orient
        stats = stat_all[pl.ds(at, n_orient)].astype(F32)
        peaks = stats[:, 0, :]
        totals = stats[:, 1, :]
        peak = jnp.max(peaks, axis=0, keepdims=True)
        total = jnp.sum(totals * jnp.exp(peaks - peak), axis=0, keepdims=True)
        if d == 0:
            evidence_ref[...] = peak + jnp.log(total)
        for side, owner in enumerate((me, partner)):
            if d > 0 and side == 1:
                shares[d, 1].wait_recv()
            scale = jnp.exp(stat_all[at + owner].astype(F32)[0:1] - peak) / total
            resp = share_all[d, side].astype(F32) * scale
            resp_all[d, side * rot_rows : (side + 1) * rot_rows] = resp.astype(BF16)
            den[side] = den[side] + jnp.sum(resp, axis=1, keepdims=True)

    share = frame_rows * n_frame / (rot_rows * n_orient)
    inverse = [1.0 / (value + share) for value in den]
    blocks = hop // width

    def spread_out(k):
        cols = slice(k * hop, (k + 1) * hop)
        mixed = jnp.dot(resp_all[0], near[:, cols], preferred_element_type=F32)
        for d in range(1, n_frame):
            mixed = mixed + jnp.dot(resp_all[d], other[d - 1, :, cols], preferred_element_type=F32)
        for side in range(2):
            value = mixed[side * rot_rows : (side + 1) * rot_rows] + share * intensity[side, :, cols]
            value = value * inverse[side]
            for b in range(blocks):
                j = k * blocks + b
                update[side, j * rot_rows : (j + 1) * rot_rows] = value[
                    :, b * width : (b + 1) * width
                ].astype(BF16)

    section = GROUP * tile_rows
    strips = section // strip

    def gather(k, c):
        deep = slice(k * blocks * rot_rows, (k + 1) * blocks * rot_rows)
        here = pl.ds(c * strips, strips)
        summed = jnp.dot(
            spread[here, :, deep].reshape(section, blocks * rot_rows),
            update[0, deep],
            preferred_element_type=F32,
        )
        return summed + jnp.dot(
            spread_pair[here, :, deep].reshape(section, blocks * rot_rows),
            update[1, deep],
            preferred_element_type=F32,
        )

    def keep(k, c):
        gathered[c] = gather(k, c) if k == 0 else gathered[c] + gather(k, c)

    def finish(away_by, own):
        c = lax.rem(me // GROUP + away_by, groups)
        summed = gather(CHUNKS - 1, c)
        if CHUNKS > 1:
            summed = summed + gathered[c]
        for i in range(GROUP):
            tile_out[c * GROUP + i] = summed[i * tile_rows : (i + 1) * tile_rows].astype(BF16)
        for i in range(1 if own else 0, GROUP):
            to = c * GROUP + lax.rem(place_in + i, GROUP)
            remote(
                tile_out.at[to],
                tile_in.at[lax.rem(to - me + n_orient, n_orient) - 1],
                fan_send.at[1],
                fan_recv.at[1],
                {"orient": to},
            ).start()

    def sections(body):
        if groups <= 4:
            for c in range(groups):
                body(c)
        else:

            def step(c, carry):
                body(c)
                return carry

            lax.fori_loop(0, groups, step, 0)

    arrived(0)
    spread_out(0)
    for k in range(1, CHUNKS):
        arrived(k)
        spread_out(k)
        sections(lambda c: keep(k - 1, c))
    each(list(range(1, groups)), lambda c: finish(c, False))
    finish(0, True)

    prior_weight = rot_rows * group_blocks / (4.0 * tile_rows)
    pltpu.make_async_copy(sums_in, sums_in, fan_recv.at[3]).wait()
    packed = lax.fori_loop(
        0, n_orient - 1, lambda d, so_far: so_far + sums_in[d].astype(F32), sums[me].astype(F32)
    )
    weight = jnp.concatenate(
        [packed[:, b : b + 1] + packed[:, 64 + b : 65 + b] for b in range(tile_rows // 8)], axis=0
    )
    weight = 1.0 / (weight + prior_weight)
    prior = prior_weight * prior_ref[0] + tile_out[me].astype(F32)
    both = weight_low[0] + weight_low[1]
    both = jnp.where(index[0] == index[1], both.astype(BF16).astype(F32), both)
    scale = 1.0 / both
    for copy in pair_copies:
        copy.wait_send()
    pltpu.make_async_copy(other, other, count_send.at[0]).wait()
    for copy in shares.values():
        copy.wait_send()
    pltpu.make_async_copy(stats_there, stats_there, fan_send.at[0]).wait()
    pltpu.make_async_copy(sums_in, sums_in, fan_send.at[3]).wait()

    pltpu.make_async_copy(tile_in, tile_in, fan_recv.at[1]).wait()
    whole = lax.fori_loop(
        0, n_orient - 1, lambda d, so_far: so_far + tile_in[d].astype(F32), prior
    )
    value = whole * weight
    volume_ref[0] = value
    tiles[me] = (value - 1.0).astype(BF16)

    def send_volume(d):
        where = tiles.at[me]
        remote(
            where, where, fan_send.at[2], fan_recv.at[2], {"orient": lax.rem(me + d, n_orient)}
        ).start()

    each(far_first(n_orient), send_volume)

    pltpu.make_async_copy(tile_in, tile_in, fan_send.at[1]).wait()
    incoming = tiles.at[pl.ds(0, n_orient - 1)]
    pltpu.make_async_copy(incoming, incoming, fan_recv.at[2]).wait()
    owners = chunk // tile_rows

    def turn(c, carry):
        value = tiles[pl.ds(c * owners, owners)].astype(F32).reshape(chunk, width)
        tiles_t[:, pl.ds(pl.multiple_of(c * chunk, 128), chunk)] = value.T.astype(BF16)
        return carry

    lax.fori_loop(0, tile_count // chunk, turn, 0)
    pair = 2 if half_blocks % 2 == 0 else 1
    for c in range(group_blocks // pair):
        cols = slice(c * pair * rot_rows, (c + 1) * pair * rot_rows)
        block = spread[:, :, cols].reshape(tile_count, pair * rot_rows)
        blended = jnp.dot(tiles_t[...], block, preferred_element_type=F32)
        for k in range(pair):
            j = c * pair + k
            value = blended[:, k * rot_rows : (k + 1) * rot_rows] * scale[j][None, :]
            value = jnp.log(1.0 + value)
            where = lax.rem(core * half_blocks + j, group_blocks) * width
            new_log_ref[:, pl.ds(pl.multiple_of(where, 128), width)] = value.T.astype(BF16)
    pltpu.make_async_copy(incoming, incoming, fan_send.at[2]).wait()


def place(a_in, b_in, c_in, a_out, b_out, c_out, sem):
    copies = [
        pltpu.make_async_copy(source, target, sem.at[i])
        for i, (source, target) in enumerate(((a_in, a_out), (b_in, b_out), (c_in, c_out)))
    ]
    for copy in copies:
        copy.start()
    for copy in copies:
        copy.wait()


def on_device(log_tomograms, frames, tile_index, tile_weight, prior_volume):
    n_orient = lax.axis_size("orient")
    n_frame = lax.axis_size("frame")
    rot_rows, pixels = log_tomograms.shape
    frame_rows = frames.shape[0]
    group_blocks = tile_index.shape[1]
    tile_rows, width = prior_volume.shape[1:]
    columns = pixels // n_frame
    tile_count = tile_rows * n_orient
    others = max(n_frame - 1, 1)
    half = columns // 2
    chunk = (384 // tile_rows if n_orient % max(384 // tile_rows, 1) == 0 else 1) * tile_rows
    dma = pltpu.SemaphoreType.DMA
    vmem = pl.BlockSpec(memory_space=pltpu.VMEM)
    hbm = pl.BlockSpec(memory_space=pltpu.HBM)
    new_log, volume, evidence = pl.pallas_call(
        functools.partial(kernel, n_orient, n_frame),
        out_shape=(
            pltpu.VMEM((rot_rows, columns), BF16),
            pltpu.VMEM((1, tile_rows, width), F32),
            pltpu.VMEM((1, frame_rows), F32),
        ),
        in_specs=[hbm] * 5,
        out_specs=(vmem, vmem, vmem),
        scratch_shapes=[
            pltpu.VMEM((n_frame, 2, rot_rows, half), BF16),
            pltpu.VMEM((rot_rows, half), BF16),
            pltpu.VMEM((n_frame, 2, frame_rows, half), jnp.int32),
            pltpu.VMEM(tile_index.shape, jnp.int32),
            pltpu.VMEM(tile_index.shape, jnp.int32),
            pltpu.VMEM(tile_weight.shape, F32),
            pltpu.VMEM(tile_weight.shape, F32),
            pltpu.VMEM(prior_volume.shape, F32),
            pltpu.VMEM((others, frame_rows, half), BF16),
            pltpu.VMEM((frame_rows, half), BF16),
            pltpu.VMEM((others, frame_rows, half), BF16),
            pltpu.VMEM((2, rot_rows, half), F32),
            pltpu.VMEM((n_frame, 2, rot_rows, frame_rows), BF16),
            pltpu.VMEM((n_frame * n_orient, 2, frame_rows), BF16),
            pltpu.VMEM((n_frame, 2 * rot_rows, frame_rows), BF16),
            pltpu.VMEM((n_orient // 2, 2 * tile_rows, group_blocks * rot_rows), BF16),
            pltpu.VMEM((n_orient // 2, 2 * tile_rows, group_blocks // 2 * rot_rows), BF16),
            pltpu.VMEM((2, group_blocks // 2 * rot_rows, width), BF16),
            pltpu.VMEM((n_orient, 8, width), BF16),
            pltpu.VMEM((n_orient - 1, 8, width), BF16),
            pltpu.VMEM((n_orient // GROUP, GROUP * tile_rows, width), F32),
            pltpu.VMEM((n_orient, tile_rows, width), BF16),
            pltpu.VMEM((n_orient - 1, tile_rows, width), BF16),
            pltpu.VMEM((n_orient, tile_rows, width), BF16),
            pltpu.VMEM((width, tile_count), BF16),
            dma((6, max(n_frame, 2))),
            pltpu.SemaphoreType.REGULAR((1,)),
            dma((1,)),
            dma((3, others, CHUNKS)),
            dma((3,)),
            dma((3,)),
            dma((n_frame, 2)),
            dma((n_frame, 2)),
            dma((4,)),
            dma((4,)),
        ],
        compiler_params=pltpu.CompilerParams(
            collective_id=0, has_side_effects=True, vmem_limit_bytes=48 * 1024 * 1024
        ),
    )(*(
        pltpu.with_memory_space_constraint(value, pltpu.HBM)
        for value in (log_tomograms, frames, tile_index, tile_weight, prior_volume)
    ))
    made = (new_log, volume, evidence)
    new_log, volume, evidence = pl.pallas_call(
        place,
        out_shape=tuple(jax.ShapeDtypeStruct(value.shape, value.dtype) for value in made),
        in_specs=[vmem] * 3,
        out_specs=(hbm,) * 3,
        scratch_shapes=[dma((3,))],
        compiler_params=pltpu.CompilerParams(vmem_limit_bytes=4 * 1024 * 1024),
    )(*made)
    return (new_log, volume, evidence.reshape(frame_rows))


def solution(mesh):
    placed = (
        P("orient", None),
        P("frame", None),
        P(None, "frame", "orient"),
        P(None, "frame", "orient"),
        P("frame", "orient", None),
    )
    return jax.shard_map(
        on_device,
        mesh=mesh,
        in_specs=placed,
        out_specs=(P("orient", "frame"), P("frame", "orient", None), P("frame")),
        check_vma=False,
    )
```

```python
import functools

import jax
import jax.numpy as jnp
from jax import lax
from jax.experimental import pallas as pl
from jax.experimental.pallas import tpu as pltpu
from jax.sharding import PartitionSpec as P

MESH = pl.DeviceIdType.MESH
F32 = jnp.float32
BF16 = jnp.bfloat16
GROUP = 8
CHUNKS = 2


def remote(src, dst, send_sem, recv_sem, where):
    return pltpu.make_async_remote_copy(
        src_ref=src,
        dst_ref=dst,
        send_sem=send_sem,
        recv_sem=recv_sem,
        device_id=where,
        device_id_type=MESH,
    )


def each(order, body):
    if len(order) <= 32:
        for d in order:
            body(d)
    else:

        def step(d, carry):
            body(d)
            return carry

        lax.fori_loop(1, len(order) + 1, step, 0)


def kernel(
    n_orient,
    n_frame,
    logt_hbm,
    frames_hbm,
    index_hbm,
    weight_hbm,
    prior_hbm,
    new_log_ref,
    volume_ref,
    evidence_ref,
    logt,
    logt_pair,
    frames,
    index_ref,
    index_pair,
    weight_ref,
    weight_pair,
    prior_ref,
    away,
    near,
    other,
    intensity,
    share_all,
    stat_all,
    resp_all,
    spread,
    spread_pair,
    update,
    sums,
    sums_in,
    gathered,
    tile_out,
    tile_in,
    tiles,
    tiles_t,
    in_sem,
    hello,
    count_send,
    count_recv,
    pair_recv,
    share_recv,
    fan_send,
    fan_recv,
):
    me = lax.axis_index("orient")
    mine = lax.axis_index("frame")
    rot_rows = logt.shape[2]
    frame_rows = frames.shape[2]
    group_blocks = index_ref.shape[1]
    half_blocks = group_blocks // 2
    tile_rows, width = prior_ref.shape[1:]
    half = logt.shape[3]
    columns = 2 * half
    pixels = columns * n_frame
    tile_count = tile_rows * n_orient
    chunk = (384 // tile_rows if n_orient % max(384 // tile_rows, 1) == 0 else 1) * tile_rows
    quarter = frame_rows // 4
    hop = half // CHUNKS

    place_in = lax.rem(me, GROUP)
    base = me - place_in
    core = lax.rem(place_in, 2)
    low = lax.rem(place_in // 2, 2)
    high = place_in // 4
    parity = lax.rem(low + high, 2)
    partner = me + 1 - 2 * core
    beside = me + 2 - 4 * low
    above = me + 4 - 8 * high

    barrier = pltpu.get_barrier_semaphore()

    def signal(sem, where):
        pl.semaphore_signal(sem, inc=1, device_id=where, device_id_type=MESH)

    groups = n_orient // GROUP

    def greet_group(sem):
        for e in reversed(range(n_frame)):
            for bits in reversed(range(GROUP)):
                if e + bits > 0:
                    where = base + flip(bits)
                    signal(sem, {"orient": where, "frame": lax.rem(mine + e, n_frame)})

    def greet_alike(sem):
        for e in range(n_frame):
            to = lax.rem(mine + e, n_frame)
            each(
                list(range(1, groups)),
                lambda k: signal(
                    sem, {"orient": lax.rem(me + k * GROUP, n_orient), "frame": to}
                ),
            )

    def flip(bits):
        return (
            (1 - core if bits % 2 else core)
            + 2 * (1 - low if bits // 2 % 2 else low)
            + 4 * (1 - high if bits // 4 else high)
        )

    def to_group(g, body):
        first = lax.rem(me // GROUP + g, groups) * GROUP
        for bits in reversed(range(GROUP)):
            if not (isinstance(g, int) and g == 0 and bits == 0):
                body(first + flip(bits))

    def to_peers(body):
        each(list(range(1, groups)), lambda g: to_group(g, body))
        to_group(0, body)

    def slot_of(to):
        return lax.rem(to - me + n_orient, n_orient) - 1

    def rows_of(q, count=1):
        return pl.ds(pl.multiple_of(q * quarter, quarter), count * quarter)

    def columns_of(d, side):
        start = lax.rem(mine + d, n_frame) * columns + (core + side - 2 * core * side) * half
        return pl.ds(pl.multiple_of(start, 128), half)

    def source_of(d):
        return lax.rem(mine + n_frame - d, n_frame)

    def load(source, target, sem):
        copy = pltpu.make_async_copy(source, target, sem)
        copy.start()
        return copy

    mine_rows = rows_of(parity * 2, 2)
    rest_rows = rows_of(2 - parity * 2, 2)
    first_copies = [
        load(
            frames_hbm.at[mine_rows, columns_of(d, 0)],
            frames.at[d, 0, mine_rows],
            in_sem.at[0, d - 1],
        )
        for d in range(1, n_frame)
    ]
    greet_alike(barrier)
    greet_group(barrier)

    loads = {}
    for d in (*range(1, n_frame), 0):
        for side in range(2):
            first = load(
                logt_hbm.at[:, columns_of(d, side)], logt.at[d, side], in_sem.at[1 + side, d]
            )
            rows = rest_rows if d > 0 and side == 0 else pl.ds(0, frame_rows)
            rest = load(
                frames_hbm.at[rows, columns_of(d, side)],
                frames.at[d, side, rows],
                in_sem.at[3 + side, d],
            )
            loads[d, side] = (first, rest)
    small_copies = [
        load(index_hbm, index_ref, in_sem.at[5, 0]),
        load(weight_hbm, weight_ref, in_sem.at[5, 1]),
        load(prior_hbm, prior_ref, in_sem.at[0, n_frame - 1]),
    ]

    for d in range(1, n_frame):
        first_copies[d - 1].wait()
        away[d - 1, mine_rows] = frames[d, 0, mine_rows].astype(F32).astype(BF16)

    pl.semaphore_wait(barrier, groups * n_frame - n_frame + GROUP * n_frame - 1)

    relayed = rows_of(parity * 2 + low)
    kept = rows_of(parity * 2 + 1 - low)
    cross = {}

    def part_cols(k):
        return pl.ds(k * hop, hop)

    def send_across(kind, rows):
        for k in range(CHUNKS):
            for d in range(1, n_frame):
                cross[kind, k, d] = remote(
                    away.at[d - 1, rows, part_cols(k)],
                    other.at[d - 1, rows, part_cols(k)],
                    count_send.at[0],
                    count_recv.at[kind, d - 1, k],
                    {"frame": lax.rem(mine + d, n_frame)},
                )
                cross[kind, k, d].start()

    greet_group(hello.at[0])
    send_across(0, relayed)

    def relay(k):
        for d in range(1, n_frame):
            cross[0, k, d].wait_recv()
            where = other.at[d - 1, relayed, part_cols(k)]
            for to in (beside, above):
                remote(
                    where, where, count_send.at[0], count_recv.at[2, d - 1, k], {"orient": to}
                ).start()

    def arrived(k):
        for d in range(1, n_frame):
            where = other.at[d - 1, rest_rows, part_cols(k)]
            pltpu.make_async_copy(where, where, count_recv.at[2, d - 1, k]).wait()
            cross[1, k, d].wait_recv()

    mass = jnp.zeros((rot_rows, 128), F32)
    correlation = jnp.zeros((rot_rows, frame_rows), F32)
    contract = (((1,), (1,)), ((), ()))

    for d in (*range(1, n_frame), 0):
        for side in range(2):
            loads[d, side][0].wait()
            value = jnp.exp(logt[d, side].astype(F32))
            if d == 0 and side == 0:
                intensity[0] = value
            for k in range(half // 128):
                mass = mass + value[:, k * 128 : (k + 1) * 128]
            loads[d, side][1].wait()
            if d > 0 and side == 0:
                away[d - 1, rest_rows] = frames[d, 0, rest_rows].astype(F32).astype(BF16)
                counts = away[d - 1]
            else:
                counts = frames[d, side].astype(F32).astype(BF16)
                if d == 0 and side == 0:
                    near[...] = counts
            correlation = correlation + lax.dot_general(
                logt[d, side], counts, contract, preferred_element_type=F32
            )

    score = (64.0 / pixels) * (correlation - jnp.sum(mass, axis=1, keepdims=True))
    peak = jnp.max(score, axis=0, keepdims=True).astype(BF16)
    grown = jnp.exp(score - peak.astype(F32))
    share_all[0, 0] = grown.astype(BF16)
    here = mine * n_orient + me
    total = jnp.sum(grown, axis=0, keepdims=True).astype(BF16)
    stat_all[here] = jnp.concatenate([peak, total], axis=0)
    def send_share(d, side, to):
        copy = remote(
            share_all.at[0 if side == 0 or d == 0 else d, 0],
            share_all.at[d, side],
            in_sem.at[3 + side, d],
            share_recv.at[d, side],
            to,
        )
        copy.start()
        return copy

    shares = {
        (d, 0): send_share(d, 0, {"frame": lax.rem(mine + d, n_frame)})
        for d in range(1, n_frame)
    }
    shares[0, 1] = send_share(0, 1, {"orient": partner})
    pl.semaphore_wait(hello.at[0], GROUP * n_frame - 1)

    def send_stat(to, frame):
        remote(
            stat_all.at[here],
            stat_all.at[here],
            fan_send.at[0],
            fan_recv.at[0],
            {"orient": to, "frame": frame},
        ).start()

    for e in range(1, n_frame):
        frame = lax.rem(mine + e, n_frame)
        to_peers(lambda to: send_stat(to, frame))
        send_stat(me, frame)
    to_peers(lambda to: send_stat(to, mine))

    send_across(1, kept)
    for copy in small_copies:
        copy.wait()
    pair_copies = []
    for i, (source, target) in enumerate(
        ((index_ref, index_pair), (weight_ref, weight_pair), (logt.at[0, 1], logt_pair))
    ):
        copy = remote(source, target, in_sem.at[i + 1, 0], pair_recv.at[i], {"orient": partner})
        copy.start()
        pair_copies.append(copy)

    def swap(value):
        turned = jnp.concatenate([value[:, half_blocks:], value[:, :half_blocks]], axis=1)
        return jnp.where(core == 0, value, turned)

    index = swap(index_ref[...])
    weight_low = swap(weight_ref[...].astype(BF16).astype(F32))
    lane = lax.broadcasted_iota(jnp.int32, (8, 128), 1)
    joint = spread.shape[1] // tile_rows
    strip = joint * tile_rows

    def hits(row_id, index, weight, j):
        value = jnp.where(row_id == index[0, j][None, :], weight[0, j][None, :], 0.0)
        value = value + jnp.where(row_id == index[1, j][None, :], weight[1, j][None, :], 0.0)
        return value.astype(BF16)

    def build(o, carry):
        row_id = lax.broadcasted_iota(jnp.int32, (strip, rot_rows), 0) + o * strip
        total = jnp.zeros((strip, rot_rows), F32)
        for j in range(group_blocks):
            narrow = hits(row_id, index, weight_low, j)
            total = total + narrow.astype(F32)
            spread[o, :, j * rot_rows : (j + 1) * rot_rows] = narrow
        weight_sum = jnp.sum(total, axis=1, keepdims=True)
        for i in range(joint):
            packed = jnp.zeros((8, 128), F32)
            for b in range(tile_rows // 8):
                at = i * tile_rows + b * 8
                exact = weight_sum[at : at + 8]
                upper = exact.astype(BF16).astype(F32)
                packed = packed + jnp.where(lane == b, upper, 0.0)
                packed = packed + jnp.where(lane == 64 + b, exact - upper, 0.0)
            sums[o * joint + i] = packed.astype(BF16)
        return carry

    builds = n_orient // joint
    for k in range(CHUNKS):
        lax.fori_loop(k * builds // CHUNKS, (k + 1) * builds // CHUNKS, build, 0)
        relay(k)

    def send_sums(to):
        remote(
            sums.at[to], sums_in.at[slot_of(to)], fan_send.at[3], fan_recv.at[3], {"orient": to}
        ).start()

    to_peers(send_sums)

    for copy in pair_copies:
        copy.wait_recv()
    index_two = jnp.where(core == 0, index_pair[:, :half_blocks], index_pair[:, half_blocks:])
    weight_two = jnp.where(core == 0, weight_pair[:, :half_blocks], weight_pair[:, half_blocks:])
    weight_two = weight_two.astype(BF16).astype(F32)
    intensity[1] = jnp.exp(logt_pair[...].astype(F32))

    def build_pair(o, carry):
        row_id = lax.broadcasted_iota(jnp.int32, (strip, rot_rows), 0) + o * strip
        for j in range(half_blocks):
            spread_pair[o, :, j * rot_rows : (j + 1) * rot_rows] = hits(
                row_id, index_two, weight_two, j
            )
        return carry

    lax.fori_loop(0, builds, build_pair, 0)

    for d in range(1, n_frame):
        shares[d, 0].wait_recv()
        shares[d, 1] = send_share(d, 1, {"orient": partner})

    stats_there = stat_all.at[pl.ds(0, n_orient * n_frame - 1)]
    pltpu.make_async_copy(stats_there, stats_there, fan_recv.at[0]).wait()
    shares[0, 1].wait_recv()
    den = [jnp.zeros((rot_rows, 1), F32) for _ in range(2)]
    for d in range(n_frame):
        at = source_of(d) * n_orient
        stats = stat_all[pl.ds(at, n_orient)].astype(F32)
        peaks = stats[:, 0, :]
        totals = stats[:, 1, :]
        peak = jnp.max(peaks, axis=0, keepdims=True)
        total = jnp.sum(totals * jnp.exp(peaks - peak), axis=0, keepdims=True)
        if d == 0:
            evidence_ref[...] = peak + jnp.log(total)
        for side, owner in enumerate((me, partner)):
            if d > 0 and side == 1:
                shares[d, 1].wait_recv()
            scale = jnp.exp(stat_all[at + owner].astype(F32)[0:1] - peak) / total
            resp = share_all[d, side].astype(F32) * scale
            resp_all[d, side * rot_rows : (side + 1) * rot_rows] = resp.astype(BF16)
            den[side] = den[side] + jnp.sum(resp, axis=1, keepdims=True)

    share = frame_rows * n_frame / (rot_rows * n_orient)
    inverse = [1.0 / (value + share) for value in den]
    blocks = hop // width

    def spread_out(k):
        cols = slice(k * hop, (k + 1) * hop)
        mixed = jnp.dot(resp_all[0], near[:, cols], preferred_element_type=F32)
        for d in range(1, n_frame):
            mixed = mixed + jnp.dot(resp_all[d], other[d - 1, :, cols], preferred_element_type=F32)
        for side in range(2):
            value = mixed[side * rot_rows : (side + 1) * rot_rows] + share * intensity[side, :, cols]
            value = value * inverse[side]
            for b in range(blocks):
                j = k * blocks + b
                update[side, j * rot_rows : (j + 1) * rot_rows] = value[
                    :, b * width : (b + 1) * width
                ].astype(BF16)

    section = GROUP * tile_rows
    strips = section // strip

    def gather(k, c):
        deep = slice(k * blocks * rot_rows, (k + 1) * blocks * rot_rows)
        here = pl.ds(c * strips, strips)
        summed = jnp.dot(
            spread[here, :, deep].reshape(section, blocks * rot_rows),
            update[0, deep],
            preferred_element_type=F32,
        )
        return summed + jnp.dot(
            spread_pair[here, :, deep].reshape(section, blocks * rot_rows),
            update[1, deep],
            preferred_element_type=F32,
        )

    def keep(k, c):
        gathered[c] = gather(k, c) if k == 0 else gathered[c] + gather(k, c)

    def finish(away_by):
        c = lax.rem(me // GROUP + away_by, groups)
        summed = gather(CHUNKS - 1, c)
        if CHUNKS > 1:
            summed = summed + gathered[c]
        for i in range(GROUP):
            tile_out[c * GROUP + i] = summed[i * tile_rows : (i + 1) * tile_rows].astype(BF16)
        def send_tiles(to):
            remote(
                tile_out.at[to],
                tile_in.at[slot_of(to)],
                fan_send.at[1],
                fan_recv.at[1],
                {"orient": to},
            ).start()

        to_group(away_by, send_tiles)

    def sections(body):
        if groups <= 4:
            for c in range(groups):
                body(c)
        else:

            def step(c, carry):
                body(c)
                return carry

            lax.fori_loop(0, groups, step, 0)

    arrived(0)
    spread_out(0)
    for k in range(1, CHUNKS):
        arrived(k)
        spread_out(k)
        sections(lambda c: keep(k - 1, c))
    each(list(range(1, groups)), finish)
    finish(0)

    prior_weight = rot_rows * group_blocks / (4.0 * tile_rows)
    pltpu.make_async_copy(sums_in, sums_in, fan_recv.at[3]).wait()
    packed = lax.fori_loop(
        0, n_orient - 1, lambda d, so_far: so_far + sums_in[d].astype(F32), sums[me].astype(F32)
    )
    weight = jnp.concatenate(
        [packed[:, b : b + 1] + packed[:, 64 + b : 65 + b] for b in range(tile_rows // 8)], axis=0
    )
    weight = 1.0 / (weight + prior_weight)
    prior = prior_weight * prior_ref[0] + tile_out[me].astype(F32)
    both = weight_low[0] + weight_low[1]
    both = jnp.where(index[0] == index[1], both.astype(BF16).astype(F32), both)
    scale = 1.0 / both
    for copy in pair_copies:
        copy.wait_send()
    pltpu.make_async_copy(other, other, count_send.at[0]).wait()
    for copy in shares.values():
        copy.wait_send()
    pltpu.make_async_copy(stats_there, stats_there, fan_send.at[0]).wait()
    pltpu.make_async_copy(sums_in, sums_in, fan_send.at[3]).wait()

    pltpu.make_async_copy(tile_in, tile_in, fan_recv.at[1]).wait()
    whole = lax.fori_loop(
        0, n_orient - 1, lambda d, so_far: so_far + tile_in[d].astype(F32), prior
    )
    value = whole * weight
    volume_ref[0] = value
    tiles[me] = (value - 1.0).astype(BF16)

    def send_volume(to):
        where = tiles.at[me]
        remote(where, where, fan_send.at[2], fan_recv.at[2], {"orient": to}).start()

    to_peers(send_volume)

    pltpu.make_async_copy(tile_in, tile_in, fan_send.at[1]).wait()
    incoming = tiles.at[pl.ds(0, n_orient - 1)]
    pltpu.make_async_copy(incoming, incoming, fan_recv.at[2]).wait()
    owners = chunk // tile_rows

    def turn(c, carry):
        value = tiles[pl.ds(c * owners, owners)].astype(F32).reshape(chunk, width)
        tiles_t[:, pl.ds(pl.multiple_of(c * chunk, 128), chunk)] = value.T.astype(BF16)
        return carry

    lax.fori_loop(0, tile_count // chunk, turn, 0)
    pair = 2 if half_blocks % 2 == 0 else 1
    for c in range(group_blocks // pair):
        cols = slice(c * pair * rot_rows, (c + 1) * pair * rot_rows)
        block = spread[:, :, cols].reshape(tile_count, pair * rot_rows)
        blended = jnp.dot(tiles_t[...], block, preferred_element_type=F32)
        for k in range(pair):
            j = c * pair + k
            value = blended[:, k * rot_rows : (k + 1) * rot_rows] * scale[j][None, :]
            value = jnp.log(1.0 + value)
            where = lax.rem(core * half_blocks + j, group_blocks) * width
            new_log_ref[:, pl.ds(pl.multiple_of(where, 128), width)] = value.T.astype(BF16)
    pltpu.make_async_copy(incoming, incoming, fan_send.at[2]).wait()


def place(a_in, b_in, c_in, a_out, b_out, c_out, sem):
    copies = [
        pltpu.make_async_copy(source, target, sem.at[i])
        for i, (source, target) in enumerate(((a_in, a_out), (b_in, b_out), (c_in, c_out)))
    ]
    for copy in copies:
        copy.start()
    for copy in copies:
        copy.wait()


def on_device(log_tomograms, frames, tile_index, tile_weight, prior_volume):
    n_orient = lax.axis_size("orient")
    n_frame = lax.axis_size("frame")
    rot_rows, pixels = log_tomograms.shape
    frame_rows = frames.shape[0]
    group_blocks = tile_index.shape[1]
    tile_rows, width = prior_volume.shape[1:]
    columns = pixels // n_frame
    tile_count = tile_rows * n_orient
    others = max(n_frame - 1, 1)
    half = columns // 2
    chunk = (384 // tile_rows if n_orient % max(384 // tile_rows, 1) == 0 else 1) * tile_rows
    dma = pltpu.SemaphoreType.DMA
    vmem = pl.BlockSpec(memory_space=pltpu.VMEM)
    hbm = pl.BlockSpec(memory_space=pltpu.HBM)
    new_log, volume, evidence = pl.pallas_call(
        functools.partial(kernel, n_orient, n_frame),
        out_shape=(
            pltpu.VMEM((rot_rows, columns), BF16),
            pltpu.VMEM((1, tile_rows, width), F32),
            pltpu.VMEM((1, frame_rows), F32),
        ),
        in_specs=[hbm] * 5,
        out_specs=(vmem, vmem, vmem),
        scratch_shapes=[
            pltpu.VMEM((n_frame, 2, rot_rows, half), BF16),
            pltpu.VMEM((rot_rows, half), BF16),
            pltpu.VMEM((n_frame, 2, frame_rows, half), jnp.int32),
            pltpu.VMEM(tile_index.shape, jnp.int32),
            pltpu.VMEM(tile_index.shape, jnp.int32),
            pltpu.VMEM(tile_weight.shape, F32),
            pltpu.VMEM(tile_weight.shape, F32),
            pltpu.VMEM(prior_volume.shape, F32),
            pltpu.VMEM((others, frame_rows, half), BF16),
            pltpu.VMEM((frame_rows, half), BF16),
            pltpu.VMEM((others, frame_rows, half), BF16),
            pltpu.VMEM((2, rot_rows, half), F32),
            pltpu.VMEM((n_frame, 2, rot_rows, frame_rows), BF16),
            pltpu.VMEM((n_frame * n_orient, 2, frame_rows), BF16),
            pltpu.VMEM((n_frame, 2 * rot_rows, frame_rows), BF16),
            pltpu.VMEM((n_orient // 2, 2 * tile_rows, group_blocks * rot_rows), BF16),
            pltpu.VMEM((n_orient // 2, 2 * tile_rows, group_blocks // 2 * rot_rows), BF16),
            pltpu.VMEM((2, group_blocks // 2 * rot_rows, width), BF16),
            pltpu.VMEM((n_orient, 8, width), BF16),
            pltpu.VMEM((n_orient - 1, 8, width), BF16),
            pltpu.VMEM((n_orient // GROUP, GROUP * tile_rows, width), F32),
            pltpu.VMEM((n_orient, tile_rows, width), BF16),
            pltpu.VMEM((n_orient - 1, tile_rows, width), BF16),
            pltpu.VMEM((n_orient, tile_rows, width), BF16),
            pltpu.VMEM((width, tile_count), BF16),
            dma((6, max(n_frame, 2))),
            pltpu.SemaphoreType.REGULAR((1,)),
            dma((1,)),
            dma((3, others, CHUNKS)),
            dma((3,)),
            dma((n_frame, 2)),
            dma((4,)),
            dma((4,)),
        ],
        compiler_params=pltpu.CompilerParams(
            collective_id=0, has_side_effects=True, vmem_limit_bytes=48 * 1024 * 1024
        ),
    )(*(
        pltpu.with_memory_space_constraint(value, pltpu.HBM)
        for value in (log_tomograms, frames, tile_index, tile_weight, prior_volume)
    ))
    made = (new_log, volume, evidence)
    new_log, volume, evidence = pl.pallas_call(
        place,
        out_shape=tuple(jax.ShapeDtypeStruct(value.shape, value.dtype) for value in made),
        in_specs=[vmem] * 3,
        out_specs=(hbm,) * 3,
        scratch_shapes=[dma((3,))],
        compiler_params=pltpu.CompilerParams(vmem_limit_bytes=4 * 1024 * 1024),
    )(*made)
    return (new_log, volume, evidence.reshape(frame_rows))


def solution(mesh):
    placed = (
        P("orient", None),
        P("frame", None),
        P(None, "frame", "orient"),
        P(None, "frame", "orient"),
        P("frame", "orient", None),
    )
    return jax.shard_map(
        on_device,
        mesh=mesh,
        in_specs=placed,
        out_specs=(P("orient", "frame"), P("frame", "orient", None), P("frame")),
        check_vma=False,
    )
```

```python
import functools

import jax
import jax.numpy as jnp
from jax import lax
from jax.experimental import pallas as pl
from jax.experimental.pallas import tpu as pltpu
from jax.sharding import PartitionSpec as P

MESH = pl.DeviceIdType.MESH
F32 = jnp.float32
BF16 = jnp.bfloat16
GROUP = 8
CHUNKS = 2
FIRST = 10


def remote(src, dst, send_sem, recv_sem, where):
    return pltpu.make_async_remote_copy(
        src_ref=src,
        dst_ref=dst,
        send_sem=send_sem,
        recv_sem=recv_sem,
        device_id=where,
        device_id_type=MESH,
    )


def each(order, body):
    if len(order) <= 32:
        for d in order:
            body(d)
    else:

        def step(d, carry):
            body(d)
            return carry

        lax.fori_loop(1, len(order) + 1, step, 0)


def kernel(
    n_orient,
    n_frame,
    logt_hbm,
    frames_hbm,
    index_hbm,
    weight_hbm,
    prior_hbm,
    new_log_ref,
    volume_ref,
    evidence_ref,
    logt,
    logt_pair,
    frames,
    index_ref,
    index_pair,
    weight_ref,
    weight_pair,
    prior_ref,
    away,
    near,
    other,
    intensity,
    share_all,
    stat_all,
    resp_all,
    spread,
    spread_pair,
    update,
    sums,
    sums_in,
    gathered,
    tile_out,
    tile_in,
    tiles,
    tiles_t,
    in_sem,
    hello,
    count_send,
    count_recv,
    pair_recv,
    share_recv,
    fan_send,
    fan_recv,
):
    me = lax.axis_index("orient")
    mine = lax.axis_index("frame")
    rot_rows = logt.shape[2]
    frame_rows = frames.shape[2]
    group_blocks = index_ref.shape[1]
    half_blocks = group_blocks // 2
    tile_rows, width = prior_ref.shape[1:]
    half = logt.shape[3]
    columns = 2 * half
    pixels = columns * n_frame
    tile_count = tile_rows * n_orient
    chunk = (384 // tile_rows if n_orient % max(384 // tile_rows, 1) == 0 else 1) * tile_rows
    quarter = frame_rows // 4
    first_part = -(-half * FIRST // (16 * 128)) * 128
    edges = (0, first_part, half)

    place_in = lax.rem(me, GROUP)
    base = me - place_in
    core = lax.rem(place_in, 2)
    low = lax.rem(place_in // 2, 2)
    high = place_in // 4
    parity = lax.rem(low + high, 2)
    partner = me + 1 - 2 * core
    beside = me + 2 - 4 * low
    above = me + 4 - 8 * high

    barrier = pltpu.get_barrier_semaphore()

    def signal(sem, where):
        pl.semaphore_signal(sem, inc=1, device_id=where, device_id_type=MESH)

    groups = n_orient // GROUP

    def greet_group(sem):
        for e in reversed(range(n_frame)):
            for bits in reversed(range(GROUP)):
                if e + bits > 0:
                    where = base + flip(bits)
                    signal(sem, {"orient": where, "frame": lax.rem(mine + e, n_frame)})

    def greet_alike(sem):
        for e in range(n_frame):
            to = lax.rem(mine + e, n_frame)
            each(
                list(range(1, groups)),
                lambda k: signal(
                    sem, {"orient": lax.rem(me + k * GROUP, n_orient), "frame": to}
                ),
            )

    def flip(bits):
        return (
            (1 - core if bits % 2 else core)
            + 2 * (1 - low if bits // 2 % 2 else low)
            + 4 * (1 - high if bits // 4 else high)
        )

    def to_group(g, body):
        first = lax.rem(me // GROUP + g, groups) * GROUP
        for bits in reversed(range(GROUP)):
            if not (isinstance(g, int) and g == 0 and bits == 0):
                body(first + flip(bits))

    def to_peers(body):
        each(list(range(1, groups)), lambda g: to_group(g, body))
        to_group(0, body)

    def slot_of(to):
        return lax.rem(to - me + n_orient, n_orient) - 1

    def rows_of(q, count=1):
        return pl.ds(pl.multiple_of(q * quarter, quarter), count * quarter)

    def columns_of(d, side):
        start = lax.rem(mine + d, n_frame) * columns + (core + side - 2 * core * side) * half
        return pl.ds(pl.multiple_of(start, 128), half)

    def source_of(d):
        return lax.rem(mine + n_frame - d, n_frame)

    def load(source, target, sem):
        copy = pltpu.make_async_copy(source, target, sem)
        copy.start()
        return copy

    mine_rows = rows_of(parity * 2, 2)
    rest_rows = rows_of(2 - parity * 2, 2)
    first_copies = [
        load(
            frames_hbm.at[mine_rows, columns_of(d, 0)],
            frames.at[d, 0, mine_rows],
            in_sem.at[0, d - 1],
        )
        for d in range(1, n_frame)
    ]
    greet_alike(barrier)
    greet_group(barrier)

    loads = {}
    for d in (*range(1, n_frame), 0):
        for side in range(2):
            first = load(
                logt_hbm.at[:, columns_of(d, side)], logt.at[d, side], in_sem.at[1 + side, d]
            )
            rows = rest_rows if d > 0 and side == 0 else pl.ds(0, frame_rows)
            rest = load(
                frames_hbm.at[rows, columns_of(d, side)],
                frames.at[d, side, rows],
                in_sem.at[3 + side, d],
            )
            loads[d, side] = (first, rest)
    small_copies = [
        load(index_hbm, index_ref, in_sem.at[5, 0]),
        load(weight_hbm, weight_ref, in_sem.at[5, 1]),
        load(prior_hbm, prior_ref, in_sem.at[0, n_frame - 1]),
    ]

    for d in range(1, n_frame):
        first_copies[d - 1].wait()
        away[d - 1, mine_rows] = frames[d, 0, mine_rows].astype(F32).astype(BF16)

    pl.semaphore_wait(barrier, groups * n_frame - n_frame + GROUP * n_frame - 1)

    relayed = rows_of(parity * 2 + low)
    kept = rows_of(parity * 2 + 1 - low)
    cross = {}

    def part_cols(k):
        return pl.ds(edges[k], edges[k + 1] - edges[k])

    def send_across(kind, rows):
        for k in range(CHUNKS):
            for d in range(1, n_frame):
                cross[kind, k, d] = remote(
                    away.at[d - 1, rows, part_cols(k)],
                    other.at[d - 1, rows, part_cols(k)],
                    count_send.at[0],
                    count_recv.at[kind, d - 1, k],
                    {"frame": lax.rem(mine + d, n_frame)},
                )
                cross[kind, k, d].start()

    greet_group(hello.at[0])
    send_across(0, relayed)

    def relay(k):
        for d in range(1, n_frame):
            cross[0, k, d].wait_recv()
            where = other.at[d - 1, relayed, part_cols(k)]
            for to in (beside, above):
                remote(
                    where, where, count_send.at[0], count_recv.at[2, d - 1, k], {"orient": to}
                ).start()

    def arrived(k):
        for d in range(1, n_frame):
            where = other.at[d - 1, rest_rows, part_cols(k)]
            pltpu.make_async_copy(where, where, count_recv.at[2, d - 1, k]).wait()
            cross[1, k, d].wait_recv()

    mass = jnp.zeros((rot_rows, 128), F32)
    correlation = jnp.zeros((rot_rows, frame_rows), F32)
    contract = (((1,), (1,)), ((), ()))

    for d in (*range(1, n_frame), 0):
        for side in range(2):
            loads[d, side][0].wait()
            value = jnp.exp(logt[d, side].astype(F32))
            if d == 0 and side == 0:
                intensity[0] = value
            for k in range(half // 128):
                mass = mass + value[:, k * 128 : (k + 1) * 128]
            loads[d, side][1].wait()
            if d > 0 and side == 0:
                away[d - 1, rest_rows] = frames[d, 0, rest_rows].astype(F32).astype(BF16)
                counts = away[d - 1]
            else:
                counts = frames[d, side].astype(F32).astype(BF16)
                if d == 0 and side == 0:
                    near[...] = counts
            correlation = correlation + lax.dot_general(
                logt[d, side], counts, contract, preferred_element_type=F32
            )

    score = (64.0 / pixels) * (correlation - jnp.sum(mass, axis=1, keepdims=True))
    peak = jnp.max(score, axis=0, keepdims=True).astype(BF16)
    grown = jnp.exp(score - peak.astype(F32))
    share_all[0, 0] = grown.astype(BF16)
    here = mine * n_orient + me
    total = jnp.sum(grown, axis=0, keepdims=True).astype(BF16)
    stat_all[here] = jnp.concatenate([peak, total], axis=0)
    def send_share(d, side, to):
        copy = remote(
            share_all.at[0 if side == 0 or d == 0 else d, 0],
            share_all.at[d, side],
            in_sem.at[3 + side, d],
            share_recv.at[d, side],
            to,
        )
        copy.start()
        return copy

    shares = {
        (d, 0): send_share(d, 0, {"frame": lax.rem(mine + d, n_frame)})
        for d in range(1, n_frame)
    }
    shares[0, 1] = send_share(0, 1, {"orient": partner})
    pl.semaphore_wait(hello.at[0], GROUP * n_frame - 1)

    def send_stat(to, frame):
        remote(
            stat_all.at[here],
            stat_all.at[here],
            fan_send.at[0],
            fan_recv.at[0],
            {"orient": to, "frame": frame},
        ).start()

    for e in range(1, n_frame):
        frame = lax.rem(mine + e, n_frame)
        to_peers(lambda to: send_stat(to, frame))
        send_stat(me, frame)
    to_peers(lambda to: send_stat(to, mine))

    send_across(1, kept)
    for copy in small_copies:
        copy.wait()
    pair_copies = []
    for i, (source, target) in enumerate(
        ((index_ref, index_pair), (weight_ref, weight_pair), (logt.at[0, 1], logt_pair))
    ):
        copy = remote(source, target, in_sem.at[i + 1, 0], pair_recv.at[i], {"orient": partner})
        copy.start()
        pair_copies.append(copy)

    def swap(value):
        turned = jnp.concatenate([value[:, half_blocks:], value[:, :half_blocks]], axis=1)
        return jnp.where(core == 0, value, turned)

    index = swap(index_ref[...])
    weight_low = swap(weight_ref[...].astype(BF16).astype(F32))
    lane = lax.broadcasted_iota(jnp.int32, (8, 128), 1)
    joint = spread.shape[1] // tile_rows
    strip = joint * tile_rows

    def hits(row_id, index, weight, j):
        value = jnp.where(row_id == index[0, j][None, :], weight[0, j][None, :], 0.0)
        value = value + jnp.where(row_id == index[1, j][None, :], weight[1, j][None, :], 0.0)
        return value.astype(BF16)

    def build(o, carry):
        row_id = lax.broadcasted_iota(jnp.int32, (strip, rot_rows), 0) + o * strip
        total = jnp.zeros((strip, rot_rows), F32)
        for j in range(group_blocks):
            narrow = hits(row_id, index, weight_low, j)
            total = total + narrow.astype(F32)
            spread[o, :, j * rot_rows : (j + 1) * rot_rows] = narrow
        weight_sum = jnp.sum(total, axis=1, keepdims=True)
        for i in range(joint):
            packed = jnp.zeros((8, 128), F32)
            for b in range(tile_rows // 8):
                at = i * tile_rows + b * 8
                exact = weight_sum[at : at + 8]
                upper = exact.astype(BF16).astype(F32)
                packed = packed + jnp.where(lane == b, upper, 0.0)
                packed = packed + jnp.where(lane == 64 + b, exact - upper, 0.0)
            sums[o * joint + i] = packed.astype(BF16)
        return carry

    builds = n_orient // joint
    for k in range(CHUNKS):
        lax.fori_loop(k * builds // CHUNKS, (k + 1) * builds // CHUNKS, build, 0)
        relay(k)

    def send_sums(to):
        remote(
            sums.at[to], sums_in.at[slot_of(to)], fan_send.at[3], fan_recv.at[3], {"orient": to}
        ).start()

    to_peers(send_sums)

    for copy in pair_copies:
        copy.wait_recv()
    index_two = jnp.where(core == 0, index_pair[:, :half_blocks], index_pair[:, half_blocks:])
    weight_two = jnp.where(core == 0, weight_pair[:, :half_blocks], weight_pair[:, half_blocks:])
    weight_two = weight_two.astype(BF16).astype(F32)
    intensity[1] = jnp.exp(logt_pair[...].astype(F32))

    def build_pair(o, carry):
        row_id = lax.broadcasted_iota(jnp.int32, (strip, rot_rows), 0) + o * strip
        for j in range(half_blocks):
            spread_pair[o, :, j * rot_rows : (j + 1) * rot_rows] = hits(
                row_id, index_two, weight_two, j
            )
        return carry

    lax.fori_loop(0, builds, build_pair, 0)

    for d in range(1, n_frame):
        shares[d, 0].wait_recv()
        shares[d, 1] = send_share(d, 1, {"orient": partner})

    stats_there = stat_all.at[pl.ds(0, n_orient * n_frame - 1)]
    pltpu.make_async_copy(stats_there, stats_there, fan_recv.at[0]).wait()
    shares[0, 1].wait_recv()
    den = [jnp.zeros((rot_rows, 1), F32) for _ in range(2)]
    for d in range(n_frame):
        at = source_of(d) * n_orient
        stats = stat_all[pl.ds(at, n_orient)].astype(F32)
        peaks = stats[:, 0, :]
        totals = stats[:, 1, :]
        peak = jnp.max(peaks, axis=0, keepdims=True)
        total = jnp.sum(totals * jnp.exp(peaks - peak), axis=0, keepdims=True)
        if d == 0:
            evidence_ref[...] = peak + jnp.log(total)
        for side, owner in enumerate((me, partner)):
            if d > 0 and side == 1:
                shares[d, 1].wait_recv()
            scale = jnp.exp(stat_all[at + owner].astype(F32)[0:1] - peak) / total
            resp = share_all[d, side].astype(F32) * scale
            resp_all[d, side * rot_rows : (side + 1) * rot_rows] = resp.astype(BF16)
            den[side] = den[side] + jnp.sum(resp, axis=1, keepdims=True)

    share = frame_rows * n_frame / (rot_rows * n_orient)
    inverse = [1.0 / (value + share) for value in den]

    def spread_out(k):
        cols = slice(edges[k], edges[k + 1])
        mixed = jnp.dot(resp_all[0], near[:, cols], preferred_element_type=F32)
        for d in range(1, n_frame):
            mixed = mixed + jnp.dot(resp_all[d], other[d - 1, :, cols], preferred_element_type=F32)
        for side in range(2):
            value = mixed[side * rot_rows : (side + 1) * rot_rows] + share * intensity[side, :, cols]
            value = value * inverse[side]
            for b in range((edges[k + 1] - edges[k]) // width):
                j = edges[k] // width + b
                update[side, j * rot_rows : (j + 1) * rot_rows] = value[
                    :, b * width : (b + 1) * width
                ].astype(BF16)

    section = GROUP * tile_rows
    strips = section // strip

    def gather(k, c):
        deep = slice(edges[k] // width * rot_rows, edges[k + 1] // width * rot_rows)
        depth = deep.stop - deep.start
        here = pl.ds(c * strips, strips)
        summed = jnp.dot(
            spread[here, :, deep].reshape(section, depth),
            update[0, deep],
            preferred_element_type=F32,
        )
        return summed + jnp.dot(
            spread_pair[here, :, deep].reshape(section, depth),
            update[1, deep],
            preferred_element_type=F32,
        )

    def keep(k, c):
        gathered[c] = gather(k, c) if k == 0 else gathered[c] + gather(k, c)

    def finish(away_by):
        c = lax.rem(me // GROUP + away_by, groups)
        summed = gather(CHUNKS - 1, c)
        if CHUNKS > 1:
            summed = summed + gathered[c]
        for i in range(GROUP):
            tile_out[c * GROUP + i] = summed[i * tile_rows : (i + 1) * tile_rows].astype(BF16)
        def send_tiles(to):
            remote(
                tile_out.at[to],
                tile_in.at[slot_of(to)],
                fan_send.at[1],
                fan_recv.at[1],
                {"orient": to},
            ).start()

        to_group(away_by, send_tiles)

    def sections(body):
        if groups <= 4:
            for c in range(groups):
                body(c)
        else:

            def step(c, carry):
                body(c)
                return carry

            lax.fori_loop(0, groups, step, 0)

    arrived(0)
    spread_out(0)
    for k in range(1, CHUNKS):
        arrived(k)
        spread_out(k)
        sections(lambda c: keep(k - 1, c))
    each(list(range(1, groups)), finish)
    finish(0)

    prior_weight = rot_rows * group_blocks / (4.0 * tile_rows)
    pltpu.make_async_copy(sums_in, sums_in, fan_recv.at[3]).wait()
    packed = lax.fori_loop(
        0, n_orient - 1, lambda d, so_far: so_far + sums_in[d].astype(F32), sums[me].astype(F32)
    )
    weight = jnp.concatenate(
        [packed[:, b : b + 1] + packed[:, 64 + b : 65 + b] for b in range(tile_rows // 8)], axis=0
    )
    weight = 1.0 / (weight + prior_weight)
    prior = prior_weight * prior_ref[0] + tile_out[me].astype(F32)
    both = weight_low[0] + weight_low[1]
    both = jnp.where(index[0] == index[1], both.astype(BF16).astype(F32), both)
    scale = 1.0 / both
    for copy in pair_copies:
        copy.wait_send()
    pltpu.make_async_copy(other, other, count_send.at[0]).wait()
    for copy in shares.values():
        copy.wait_send()
    pltpu.make_async_copy(stats_there, stats_there, fan_send.at[0]).wait()
    pltpu.make_async_copy(sums_in, sums_in, fan_send.at[3]).wait()

    pltpu.make_async_copy(tile_in, tile_in, fan_recv.at[1]).wait()
    if n_orient <= 32:
        whole = prior + jnp.sum(tile_in[...].astype(F32), axis=0)
    else:
        whole = lax.fori_loop(
            0, n_orient - 1, lambda d, so_far: so_far + tile_in[d].astype(F32), prior
        )
    value = whole * weight
    volume_ref[0] = value
    tiles[me] = (value - 1.0).astype(BF16)

    def send_volume(to):
        where = tiles.at[me]
        remote(where, where, fan_send.at[2], fan_recv.at[2], {"orient": to}).start()

    to_peers(send_volume)

    pltpu.make_async_copy(tile_in, tile_in, fan_send.at[1]).wait()
    incoming = tiles.at[pl.ds(0, n_orient - 1)]
    pltpu.make_async_copy(incoming, incoming, fan_recv.at[2]).wait()
    owners = chunk // tile_rows

    def turn(c, carry):
        value = tiles[pl.ds(c * owners, owners)].astype(F32).reshape(chunk, width)
        tiles_t[:, pl.ds(pl.multiple_of(c * chunk, 128), chunk)] = value.T.astype(BF16)
        return carry

    lax.fori_loop(0, tile_count // chunk, turn, 0)
    pair = 2 if half_blocks % 2 == 0 else 1
    for c in range(group_blocks // pair):
        cols = slice(c * pair * rot_rows, (c + 1) * pair * rot_rows)
        block = spread[:, :, cols].reshape(tile_count, pair * rot_rows)
        blended = jnp.dot(tiles_t[...], block, preferred_element_type=F32)
        for k in range(pair):
            j = c * pair + k
            value = blended[:, k * rot_rows : (k + 1) * rot_rows] * scale[j][None, :]
            value = jnp.log(1.0 + value)
            where = lax.rem(core * half_blocks + j, group_blocks) * width
            new_log_ref[:, pl.ds(pl.multiple_of(where, 128), width)] = value.T.astype(BF16)
    pltpu.make_async_copy(incoming, incoming, fan_send.at[2]).wait()


def place(a_in, b_in, c_in, a_out, b_out, c_out, sem):
    copies = [
        pltpu.make_async_copy(source, target, sem.at[i])
        for i, (source, target) in enumerate(((a_in, a_out), (b_in, b_out), (c_in, c_out)))
    ]
    for copy in copies:
        copy.start()
    for copy in copies:
        copy.wait()


def on_device(log_tomograms, frames, tile_index, tile_weight, prior_volume):
    n_orient = lax.axis_size("orient")
    n_frame = lax.axis_size("frame")
    rot_rows, pixels = log_tomograms.shape
    frame_rows = frames.shape[0]
    group_blocks = tile_index.shape[1]
    tile_rows, width = prior_volume.shape[1:]
    columns = pixels // n_frame
    tile_count = tile_rows * n_orient
    others = max(n_frame - 1, 1)
    half = columns // 2
    chunk = (384 // tile_rows if n_orient % max(384 // tile_rows, 1) == 0 else 1) * tile_rows
    dma = pltpu.SemaphoreType.DMA
    vmem = pl.BlockSpec(memory_space=pltpu.VMEM)
    hbm = pl.BlockSpec(memory_space=pltpu.HBM)
    new_log, volume, evidence = pl.pallas_call(
        functools.partial(kernel, n_orient, n_frame),
        out_shape=(
            pltpu.VMEM((rot_rows, columns), BF16),
            pltpu.VMEM((1, tile_rows, width), F32),
            pltpu.VMEM((1, frame_rows), F32),
        ),
        in_specs=[hbm] * 5,
        out_specs=(vmem, vmem, vmem),
        scratch_shapes=[
            pltpu.VMEM((n_frame, 2, rot_rows, half), BF16),
            pltpu.VMEM((rot_rows, half), BF16),
            pltpu.VMEM((n_frame, 2, frame_rows, half), jnp.int32),
            pltpu.VMEM(tile_index.shape, jnp.int32),
            pltpu.VMEM(tile_index.shape, jnp.int32),
            pltpu.VMEM(tile_weight.shape, F32),
            pltpu.VMEM(tile_weight.shape, F32),
            pltpu.VMEM(prior_volume.shape, F32),
            pltpu.VMEM((others, frame_rows, half), BF16),
            pltpu.VMEM((frame_rows, half), BF16),
            pltpu.VMEM((others, frame_rows, half), BF16),
            pltpu.VMEM((2, rot_rows, half), F32),
            pltpu.VMEM((n_frame, 2, rot_rows, frame_rows), BF16),
            pltpu.VMEM((n_frame * n_orient, 2, frame_rows), BF16),
            pltpu.VMEM((n_frame, 2 * rot_rows, frame_rows), BF16),
            pltpu.VMEM((n_orient // 2, 2 * tile_rows, group_blocks * rot_rows), BF16),
            pltpu.VMEM((n_orient // 2, 2 * tile_rows, group_blocks // 2 * rot_rows), BF16),
            pltpu.VMEM((2, group_blocks // 2 * rot_rows, width), BF16),
            pltpu.VMEM((n_orient, 8, width), BF16),
            pltpu.VMEM((n_orient - 1, 8, width), BF16),
            pltpu.VMEM((n_orient // GROUP, GROUP * tile_rows, width), F32),
            pltpu.VMEM((n_orient, tile_rows, width), BF16),
            pltpu.VMEM((n_orient - 1, tile_rows, width), BF16),
            pltpu.VMEM((n_orient, tile_rows, width), BF16),
            pltpu.VMEM((width, tile_count), BF16),
            dma((6, max(n_frame, 2))),
            pltpu.SemaphoreType.REGULAR((1,)),
            dma((1,)),
            dma((3, others, CHUNKS)),
            dma((3,)),
            dma((n_frame, 2)),
            dma((4,)),
            dma((4,)),
        ],
        compiler_params=pltpu.CompilerParams(
            collective_id=0, has_side_effects=True, vmem_limit_bytes=48 * 1024 * 1024
        ),
    )(*(
        pltpu.with_memory_space_constraint(value, pltpu.HBM)
        for value in (log_tomograms, frames, tile_index, tile_weight, prior_volume)
    ))
    made = (new_log, volume, evidence)
    new_log, volume, evidence = pl.pallas_call(
        place,
        out_shape=tuple(jax.ShapeDtypeStruct(value.shape, value.dtype) for value in made),
        in_specs=[vmem] * 3,
        out_specs=(hbm,) * 3,
        scratch_shapes=[dma((3,))],
        compiler_params=pltpu.CompilerParams(vmem_limit_bytes=4 * 1024 * 1024),
    )(*made)
    return (new_log, volume, evidence.reshape(frame_rows))


def solution(mesh):
    placed = (
        P("orient", None),
        P("frame", None),
        P(None, "frame", "orient"),
        P(None, "frame", "orient"),
        P("frame", "orient", None),
    )
    return jax.shard_map(
        on_device,
        mesh=mesh,
        in_specs=placed,
        out_specs=(P("orient", "frame"), P("frame", "orient", None), P("frame")),
        check_vma=False,
    )
```
